32 devices in a mesh: groups: 2 (over y), blk: 4 (over z), sum: 4 (over x, core).
Axes of the slice: x: 2, y: 2, z: 4, core: 2. Of those that a mesh axis runs over, the one named last changes fastest.
Arguments:
- queries: bfloat16 [64, 8192], P(('groups', 'blk', 'sum')), parts along dimension 0, may hold values from -120 to 120
- cached_key_rows: bfloat16 [64, 128, 1024], P(('groups', 'blk', 'sum')), parts along dimension 0, may hold values from -4 to 4
- cached_value_rows: bfloat16 [64, 128, 1024], P(('groups', 'blk', 'sum')), parts along dimension 0, may hold values from -4 to 4
- incoming_pairs: bfloat16 [64, 2, 1024], P(('groups', 'blk', 'sum')), parts along dimension 0, may hold values from -4 to 4
- cache_length: int32 [64], P(('groups', 'blk', 'sum')), parts along dimension 0, may hold values from 1 to 128, 2048 in all
- hidden: float32 [64, 5120], P(('groups', 'blk'), 'sum'), parts along dimension 0, may hold values from -20 to 20
- norm_gain: float32 [5120], P('sum'), may hold values from 0.25 to 1.75
- out_weight: bfloat16 [8192, 5120], P('blk', 'sum'), may hold values from -0.0625 to 0.0625
- gate_up_weight: bfloat16 [2, 25600, 5120], P(None, 'blk', 'sum'), may hold values from -0.078125 to 0.078125
- down_weight: bfloat16 [25600, 5120], P('blk', 'sum'), may hold values from -0.0390625 to 0.0390625
Outputs:
- layer_out: float32 [64, 5120], P(('groups', 'blk'), 'sum'), parts along dimension 0
The draws below stay inside these ranges and needn't reach their ends.
There are 2 independent parts, one for each index of `groups`. The reference program is written for one: setup_inputs(seed, part) draws one part's arguments, and reference() takes and returns one part's arrays. A program takes and returns all parts, laid end to end along the dimension named above; an argument that names none is the same for every part. Nothing has to cross between parts.
Inputs may be any that keep to these rules, and one draw needn't show every extreme that they name: `cache_length`: the lengths of a group's rows sum to 2048.
All inputs are finite; a program needn't handle non-finite values.
Results may differ from the reference program's by a relative error of at most 0.015.
Values may be sent and summed in bfloat16 or wider, within the bound.
A program may use at most 128 MiB of HBM per device.

```python
import math
import jax
import jax.numpy as jnp
import numpy as np
from jax import lax

D = 5120
QUERY_HEADS = 64
KEY_VALUE_HEADS = 8
HEAD_SIZE = 128
FF = 25600
CACHE_SLOTS = 128
GROUP_ROWS = 32
N_BLK = 4
N_SUM = 4


def attention_draws(key):
    stored_keys = jnp.clip(jax.random.normal(jax.random.fold_in(key, 11), (GROUP_ROWS, CACHE_SLOTS, KEY_VALUE_HEADS * HEAD_SIZE), jnp.float32), -4.0, 4.0)
    return stored_keys


def draw_cached_key_rows(key, part):
    return attention_draws(key).astype(jnp.bfloat16)


def draw_queries(key, part):
    drawn_result = jnp.clip(jax.random.normal(jax.random.fold_in(key, 21), (GROUP_ROWS, KEY_VALUE_HEADS, QUERY_HEADS // KEY_VALUE_HEADS, HEAD_SIZE), jnp.float32), -4.0, 4.0)
    return drawn_result.reshape(GROUP_ROWS, QUERY_HEADS * HEAD_SIZE).astype(jnp.bfloat16)


def draw_incoming_pairs(key, part):
    fresh_token = jnp.clip(jax.random.normal(jax.random.fold_in(key, 31), (GROUP_ROWS, 2, KEY_VALUE_HEADS * HEAD_SIZE), jnp.float32), -4.0, 4.0)
    return fresh_token.astype(jnp.bfloat16)


def draw_hidden(key, part):
    base = jnp.clip(jax.random.normal(jax.random.fold_in(key, 41), (GROUP_ROWS, D), jnp.float32), -4.0, 4.0)
    row_scale = jnp.exp(jax.random.uniform(jax.random.fold_in(key, 42), (GROUP_ROWS, 1), jnp.float32, math.log(0.3), math.log(3.0)))
    col_scale = jnp.exp(jax.random.uniform(jax.random.fold_in(key, 43), (1, D), jnp.float32, math.log(0.3), math.log(3.0)))
    position = jnp.arange(D).astype(jnp.float32)[None, :] / D
    rising = jnp.sqrt(1.0 + 2.0 * position)
    return (0.3 * base * row_scale * col_scale * rising).astype(jnp.float32)


def block_levels(own_key, shape, split, least, largest):
    factor_of, own = 1.0, jax.random.fold_in(own_key, 6)
    for axis_at, parts in split:
        steps = jnp.exp(jax.random.uniform(jax.random.fold_in(own, axis_at), (parts,), jnp.float32, least / len(split), largest / len(split)))
        factor_of = factor_of * jnp.repeat(steps, shape[axis_at] // parts).reshape([-1 if axis == axis_at else 1 for axis in range(len(shape))])
    return factor_of


def profile(count, total, most, skew):
    weights = [(1 << 20) // math.isqrt(grade ** skew) + 1 for grade in range(2, count + 1)]
    surplus, given = total - most - (count - 1), [1] * (count - 1)
    while surplus > 0:
        candidates = [i for i in range(count - 1) if given[i] < most]
        pool, remaining = sum([weights[i] for i in candidates]), surplus
        for i in candidates:
            addition = min(most - given[i], max(1, remaining * weights[i] // pool), surplus)
            given[i] = given[i] + addition
            surplus = surplus - addition
    return np.array([most] + given)


def uneven(own_key, count, total, reach, lean):
    if count == 2:
        one = jax.random.randint(own_key, (), max(1, total - reach), min(reach, total - 1) + 1)
        return jnp.stack([one, total - one])
    sizes = jnp.asarray(profile(count, total, reach, lean), jnp.int32)
    couples = (count - 1) // 2
    giver, sink = sizes[1:1 + 2 * couples:2], sizes[2:2 + 2 * couples:2]
    room = jnp.minimum(giver - 1, reach - sink)
    passed = jax.random.randint(jax.random.fold_in(own_key, 1), (couples,), 0, 1 << 20) % (room + 1)
    sizes = sizes.at[1:1 + 2 * couples:2].set(giver - passed).at[2:2 + 2 * couples:2].set(sink + passed)
    return sizes[jax.random.permutation(jax.random.fold_in(own_key, 2), count)]


def normal_values(stream_key, extent, deviation, bound, pieces=(), dtype=jnp.bfloat16):
    loudness = block_levels(stream_key, extent, pieces, -0.22, 0.18) if pieces else 1.0
    values = jax.random.normal(stream_key, extent, jnp.float32) * deviation * loudness
    return jnp.minimum(jnp.maximum(values, -bound), bound).astype(dtype)


def setup_inputs(seed: int = 0, part: int = 0) -> dict:
    streams_of = jax.random.split(jax.random.key(seed), 11)
    part_splits = jax.random.split(jax.random.fold_in(streams_of[10], part), 11)
    queries = draw_queries(jax.random.fold_in(jax.random.fold_in(streams_of[10], part), 71), part)
    cached_key_rows = draw_cached_key_rows(jax.random.fold_in(jax.random.fold_in(streams_of[10], part), 71), part)
    cached_value_rows = normal_values(part_splits[2], (GROUP_ROWS, CACHE_SLOTS, KEY_VALUE_HEADS * HEAD_SIZE), 1.0, 4.0, ((0, 16),))
    incoming_pairs = draw_incoming_pairs(jax.random.fold_in(jax.random.fold_in(streams_of[10], part), 71), part)
    cache_length = uneven(part_splits[4], GROUP_ROWS, GROUP_ROWS * CACHE_SLOTS // 2, CACHE_SLOTS, 2).astype(jnp.int32)
    hidden = draw_hidden(jax.random.fold_in(jax.random.fold_in(streams_of[10], part), 71), part)
    norm_gain = jnp.clip(1.0 + 0.15 * jax.random.normal(streams_of[6], (D,), jnp.float32), 0.25, 1.75)
    out_weight = normal_values(streams_of[7], (QUERY_HEADS * HEAD_SIZE, D), (QUERY_HEADS * HEAD_SIZE) ** -0.5, 0.0625, ((0, 4), (1, 4)))
    gate_up_weight = normal_values(streams_of[8], (2, FF, D), D ** -0.5, 0.078125, ((1, 4), (2, 4)))
    down_weight = normal_values(streams_of[9], (FF, D), FF ** -0.5, 0.0390625, ((0, 4), (1, 4)))
    return {"queries": queries, "cached_key_rows": cached_key_rows, "cached_value_rows": cached_value_rows, "incoming_pairs": incoming_pairs, "cache_length": cache_length, "hidden": hidden, "norm_gain": norm_gain, "out_weight": out_weight, "gate_up_weight": gate_up_weight, "down_weight": down_weight}


def attend(queries, cached_key_rows, cached_value_rows, incoming_pairs, cache_length):
    count_of_rows = queries.shape[0]
    score_scale = HEAD_SIZE ** (-0.5)
    query_head_count = queries.astype(jnp.float32).reshape(count_of_rows, KEY_VALUE_HEADS, QUERY_HEADS // KEY_VALUE_HEADS, HEAD_SIZE)
    key_head_count = cached_key_rows.astype(jnp.float32).reshape(count_of_rows, CACHE_SLOTS, KEY_VALUE_HEADS, HEAD_SIZE)
    value_head_count = cached_value_rows.astype(jnp.float32).reshape(count_of_rows, CACHE_SLOTS, KEY_VALUE_HEADS, HEAD_SIZE)
    incoming_key = incoming_pairs[:, 0].astype(jnp.float32).reshape(count_of_rows, KEY_VALUE_HEADS, HEAD_SIZE)
    incoming_value = incoming_pairs[:, 1].astype(jnp.float32).reshape(count_of_rows, KEY_VALUE_HEADS, HEAD_SIZE)
    scores = jnp.einsum('nkgd,nlkd->nkgl', query_head_count, key_head_count) * score_scale
    own_score = jnp.einsum('nkgd,nkd->nkg', query_head_count, incoming_key) * score_scale
    live_mask = jnp.arange(CACHE_SLOTS)[None, :] < cache_length[:, None]
    scores = jnp.where(live_mask[:, None, None, :], scores, -jnp.inf)
    row_max = jnp.maximum(lax.optimization_barrier(jnp.max(scores, axis=-1)), own_score)
    cache_terms = jnp.exp(scores - row_max[..., None])
    own_term = jnp.exp(own_score - row_max)
    row_total = lax.optimization_barrier(jnp.sum(cache_terms, axis=-1)) + own_term
    weights = (cache_terms / row_total[..., None]).astype(jnp.bfloat16)
    own_weight = (own_term / row_total).astype(jnp.bfloat16)
    mixed = jnp.einsum('nkgl,nlkd->nkgd', weights.astype(jnp.float32), value_head_count)
    mixed = mixed + own_weight.astype(jnp.float32)[..., None] * incoming_value[:, :, None, :]
    return mixed.astype(jnp.bfloat16).reshape(count_of_rows, QUERY_HEADS * HEAD_SIZE)

def rounded_add(running, partial_value):
    rounded = lax.optimization_barrier(partial_value.astype(jnp.bfloat16))
    return running + rounded.astype(jnp.float32)

def reference(queries, cached_key_rows, cached_value_rows, incoming_pairs, cache_length, hidden, norm_gain, out_weight, gate_up_weight, down_weight):
    attended = attend(queries, cached_key_rows, cached_value_rows, incoming_pairs, cache_length)
    head_width = QUERY_HEADS * HEAD_SIZE // N_BLK

    def add_heads(block_index, running):
        first_col = (block_index * head_width).astype(jnp.int32)
        columns = lax.dynamic_slice_in_dim(attended, first_col, head_width, 1)
        weight_rows = lax.dynamic_slice_in_dim(out_weight, first_col, head_width, 0)
        return rounded_add(running, jnp.dot(columns, weight_rows, preferred_element_type=jnp.float32))
    projected = lax.fori_loop(0, N_BLK, add_heads, jnp.zeros((GROUP_ROWS, D), jnp.float32))
    residual = hidden + projected
    inverse = lax.rsqrt(lax.optimization_barrier(jnp.sum(residual * residual, axis=1)) / D + 1e-06)
    normed = (residual * inverse[:, None] * norm_gain[None, :]).astype(jnp.bfloat16)
    part_width = D // N_SUM

    def add_gate(block_index, running):
        first_col = (block_index * part_width).astype(jnp.int32)
        features = lax.dynamic_slice_in_dim(normed, first_col, part_width, 1).astype(jnp.float32)
        weight_part = lax.dynamic_slice_in_dim(gate_up_weight, first_col, part_width, 2).astype(jnp.float32)
        return rounded_add(running, jnp.einsum('rd,gfd->rgf', features, weight_part))
    pre_activation = lax.fori_loop(0, N_SUM, add_gate, jnp.zeros((GROUP_ROWS, 2, FF), jnp.float32))
    activated = (jax.nn.silu(pre_activation[:, 0]) * pre_activation[:, 1]).astype(jnp.bfloat16)
    unit_width = FF // N_BLK

    def add_down(block_index, running):
        first_col = (block_index * unit_width).astype(jnp.int32)
        units = lax.dynamic_slice_in_dim(activated, first_col, unit_width, 1)
        weight_rows = lax.dynamic_slice_in_dim(down_weight, first_col, unit_width, 0)
        return rounded_add(running, jnp.dot(units, weight_rows, preferred_element_type=jnp.float32))
    feed_forward = lax.fori_loop(0, N_BLK, add_down, jnp.zeros((GROUP_ROWS, D), jnp.float32))
    return residual + feed_forward
```

```python
import jax
import jax.numpy as jnp
from jax import lax
from jax.experimental import pallas as pl
from jax.experimental.pallas import tpu as pltpu
from jax.sharding import PartitionSpec as P

D = 5120
QUERY_HEADS = 64
KEY_VALUE_HEADS = 8
HEAD_SIZE = 128
CACHE_SLOTS = 128


def attend_padded(queries, cached_key_rows, cached_value_rows, incoming_pairs, cache_length):
    count_of_rows = queries.shape[0]
    score_scale = HEAD_SIZE ** (-0.5)
    query_head_count = queries.reshape(
        count_of_rows, KEY_VALUE_HEADS, QUERY_HEADS // KEY_VALUE_HEADS, HEAD_SIZE
    )
    key_head_count = cached_key_rows.reshape(count_of_rows, CACHE_SLOTS, KEY_VALUE_HEADS, HEAD_SIZE)
    value_head_count = cached_value_rows.reshape(
        count_of_rows, CACHE_SLOTS, KEY_VALUE_HEADS, HEAD_SIZE
    )
    incoming_key = incoming_pairs[:, 0].reshape(count_of_rows, KEY_VALUE_HEADS, HEAD_SIZE)
    incoming_value = incoming_pairs[:, 1].reshape(count_of_rows, KEY_VALUE_HEADS, HEAD_SIZE)
    scores = (
        jnp.einsum(
            "nkgd,nlkd->nkgl", query_head_count, key_head_count, preferred_element_type=jnp.float32
        )
        * score_scale
    )
    own_score = (
        jnp.einsum(
            "nkgd,nkd->nkg", query_head_count, incoming_key, preferred_element_type=jnp.float32
        )
        * score_scale
    )
    live_mask = jnp.arange(CACHE_SLOTS)[None, :] < cache_length[:, None]
    scores = jnp.where(live_mask[:, None, None, :], scores, -jnp.inf)
    row_max = jnp.maximum(jnp.max(scores, axis=-1), own_score)
    cache_terms = jnp.exp(scores - row_max[..., None])
    own_term = jnp.exp(own_score - row_max)
    row_total = jnp.sum(cache_terms, axis=-1) + own_term
    weights = (cache_terms / row_total[..., None]).astype(jnp.bfloat16)
    own_weight = (own_term / row_total).astype(jnp.bfloat16)
    mixed = jnp.einsum(
        "nkgl,nlkd->nkgd", weights, value_head_count, preferred_element_type=jnp.float32
    )
    mixed = (
        mixed
        + own_weight.astype(jnp.float32)[..., None]
        * incoming_value.astype(jnp.float32)[:, :, None, :]
    )
    return mixed.astype(jnp.bfloat16).reshape(count_of_rows, QUERY_HEADS * HEAD_SIZE)


MESH = pl.DeviceIdType.MESH


TILE = 256


def layer_kernel(
    lengths,
    q_hbm,
    k_hbm,
    v_hbm,
    pair_hbm,
    hidden_hbm,
    gain_hbm,
    wo_hbm,
    wg_hbm,
    wd_hbm,
    out_ref,
    q_buf,
    k_buf,
    v_buf,
    pair_buf,
    hidden_buf,
    gain_buf,
    wo,
    wg,
    wd,
    q_rows,
    mixed,
    heads_all,
    heads_f32,
    proj_out,
    proj_in,
    residual,
    normed,
    squares,
    inverse,
    pre_part,
    pre_core,
    pre_sum,
    pre_send,
    pre_far,
    act,
    down_acc,
    down_out,
    down_in,
    load_sem,
    wg_sem,
    wd_sem,
    heads_send,
    heads_recv,
    proj_send,
    proj_recv,
    norm_send,
    norm_recv,
    square_send,
    square_recv,
    inverse_send,
    inverse_recv,
    core_send,
    core_recv,
    far_send,
    far_recv,
    act_send,
    act_recv,
    down_send,
    down_recv,
):
    n_blk, n_sum = lax.axis_size("blk"), lax.axis_size("sum")
    rows_here = q_buf.shape[0]
    units, columns = wd.shape
    tiles = units // TILE
    sizes = chunk_sizes(units)
    chunks = len(sizes)
    spans = [pl.ds(sum(sizes[:c]), sizes[c]) for c in range(chunks)]
    b, s = lax.axis_index("blk"), lax.axis_index("sum")
    core = lax.rem(s, 2)
    core_peer = s + 1 - 2 * core
    far_peer = lax.rem(s + 2, n_sum)

    def blk_peer(k):
        return lax.rem(b + k, n_blk)

    def sum_peer(k):
        return lax.rem(s + k, n_sum)

    def send(src, dst, send_sem, recv_sem, where):
        return pltpu.make_async_remote_copy(
            src_ref=src,
            dst_ref=dst,
            send_sem=send_sem,
            recv_sem=recv_sem,
            device_id=where,
            device_id_type=MESH,
        )

    blk_order = [n_blk // 2] + [k for k in range(1, n_blk) if k != n_blk // 2]
    peers = [(i, j) for i in blk_order + [0] for j in (2, 3, 1, 0) if (i, j) != (0, 0)]

    barrier = pltpu.get_barrier_semaphore()
    first = [
        pltpu.make_async_copy(src, dst, load_sem.at[i])
        for i, (src, dst) in enumerate(
            [
                (q_hbm, q_buf),
                (k_hbm, k_buf),
                (pair_hbm, pair_buf),
                (v_hbm, v_buf),
                (hidden_hbm, hidden_buf),
                (gain_hbm, gain_buf),
                (wo_hbm, wo),
            ]
        )
    ]

    def load_gate(t):
        span = pl.ds(pl.multiple_of(t * TILE, TILE), TILE)
        return pltpu.make_async_copy(wg_hbm.at[:, span, :], wg.at[:, span, :], wg_sem.at[t])

    load_down = [
        pltpu.make_async_copy(wd_hbm.at[spans[c], :], wd.at[spans[c], :], wd_sem.at[c])
        for c in range(chunks)
    ]
    for copy in first[:4]:
        copy.start()
    for i, j in peers:
        pl.semaphore_signal(
            barrier,
            inc=1,
            device_id={"blk": blk_peer(i), "sum": sum_peer(j)},
            device_id_type=MESH,
        )
    for copy in first[:4]:
        copy.wait()
    first[4].start()
    first[5].start()
    turns = turn_counts(tiles)
    for t in range(tiles):
        if t == turns[0] - 2:
            first[6].start()
        load_gate(t).start()
    for copy in load_down:
        copy.start()

    group = QUERY_HEADS // KEY_VALUE_HEADS
    queries = q_buf[...].astype(jnp.float32)
    for r in range(rows_here):
        for h in range(QUERY_HEADS):
            q_rows[r, h : h + 1, :] = queries[r : r + 1, h * HEAD_SIZE : (h + 1) * HEAD_SIZE]
    score_scale = HEAD_SIZE ** (-0.5)
    staged = []
    for r in range(rows_here):
        q32 = q_rows[r]
        q16 = q32.astype(jnp.bfloat16)
        new_key = pair_buf[r, 0:1, :].astype(jnp.float32)
        new_value = pair_buf[r, 1:2, :].astype(jnp.float32)
        scores, keys_new, values_new = [], [], []
        for j in range(KEY_VALUE_HEADS):
            cols = slice(j * HEAD_SIZE, (j + 1) * HEAD_SIZE)
            scores.append(
                lax.dot_general(
                    q16[j * group : (j + 1) * group],
                    k_buf[r, :, cols],
                    (((1,), (1,)), ((), ())),
                    preferred_element_type=jnp.float32,
                )
            )
            keys_new.append(jnp.broadcast_to(new_key[:, cols], (group, HEAD_SIZE)))
            values_new.append(jnp.broadcast_to(new_value[:, cols], (group, HEAD_SIZE)))
        scores = jnp.concatenate(scores, axis=0) * score_scale
        own = jnp.sum(q32 * jnp.concatenate(keys_new, axis=0), axis=1, keepdims=True) * score_scale
        staged.append((scores, own, jnp.concatenate(values_new, axis=0)))
    weighted = []
    for r in range(rows_here):
        scores, own, _ = staged[r]
        position = lax.broadcasted_iota(jnp.int32, scores.shape, 1)
        scores = jnp.where(position < lengths[r], scores, -jnp.inf)
        row_max = jnp.maximum(jnp.max(scores, axis=1, keepdims=True), own)
        terms = jnp.exp(scores - row_max)
        own_term = jnp.exp(own - row_max)
        total = jnp.sum(terms, axis=1, keepdims=True) + own_term
        weights = (terms / total).astype(jnp.bfloat16)
        weighted.append((weights, (own_term / total).astype(jnp.bfloat16).astype(jnp.float32)))
    for r in range(rows_here):
        weights, own_weight = weighted[r]
        outs = []
        for j in range(KEY_VALUE_HEADS):
            cols = slice(j * HEAD_SIZE, (j + 1) * HEAD_SIZE)
            outs.append(
                jnp.dot(
                    weights[j * group : (j + 1) * group],
                    v_buf[r, :, cols],
                    preferred_element_type=jnp.float32,
                )
            )
        result = jnp.concatenate(outs, axis=0) + own_weight * staged[r][2]
        mixed[r] = result.astype(jnp.bfloat16).reshape(mixed.shape[1:])

    pl.semaphore_wait(barrier, len(peers))
    moves = []
    for n, (i, j) in enumerate(peers):
        moves.append(
            send(
                mixed.at[:, blk_peer(i)],
                heads_all.at[b, s],
                heads_send.at[n],
                heads_recv.at[n],
                {"blk": blk_peer(i), "sum": sum_peer(j)},
            )
        )
    for copy in moves:
        copy.start()
    heads_all[b, s] = mixed[:, b]

    def turn(t, carry):
        load_gate(t).wait()
        span = pl.ds(pl.multiple_of(t * TILE, TILE), TILE)
        for g in range(2):
            for f in range(columns // TILE):
                cols = slice(f * TILE, (f + 1) * TILE)
                wg[g, span, cols] = wg[g, span, cols].T
        return carry

    lax.fori_loop(0, turns[0], turn, 0)
    for n, (i, j) in enumerate(peers):
        moves[n].wait_send()
        other_b, other_s = lax.rem(b + n_blk - i, n_blk), lax.rem(s + n_sum - j, n_sum)
        send(
            mixed.at[:, blk_peer(i)],
            heads_all.at[other_b, other_s],
            heads_send.at[n],
            heads_recv.at[n],
            {"blk": blk_peer(i), "sum": sum_peer(j)},
        ).wait_recv()
    heads_f32[...] = heads_all[...].astype(jnp.float32).reshape(heads_f32.shape)
    per_block = wo.shape[0] // HEAD_SIZE
    rows_all = n_blk * n_sum * rows_here
    picked = jnp.concatenate(
        [
            heads_f32[pl.ds(h, rows_all, stride=per_block), :].astype(jnp.bfloat16)
            for h in range(per_block)
        ],
        axis=1,
    )
    first[6].wait()
    projected = jnp.dot(picked, wo[...], preferred_element_type=jnp.float32)
    proj_out[...] = projected.reshape(proj_out.shape).astype(jnp.bfloat16)
    moves = [
        send(
            proj_out.at[blk_peer(k)],
            proj_in.at[k - 1],
            proj_send.at[k - 1],
            proj_recv.at[k - 1],
            {"blk": blk_peer(k)},
        )
        for k in range(1, n_blk)
    ]
    for copy in moves:
        copy.start()
    lax.fori_loop(turns[0], turns[1], turn, 0)
    first[4].wait()
    first[5].wait()
    total = hidden_buf[...] + proj_out[b].astype(jnp.float32)
    for k in range(1, n_blk):
        moves[k - 1].wait()
        total = total + proj_in[k - 1].astype(jnp.float32)
    residual[...] = total
    scaled = [
        total[:, n * 128 : (n + 1) * 128] * gain_buf[n : n + 1, :] for n in range(columns // 128)
    ]
    normed[b] = jnp.concatenate(scaled, axis=1).astype(jnp.bfloat16)
    norm_moves = [
        send(
            normed.at[b],
            normed.at[b],
            norm_send.at[k - 1],
            norm_recv.at[k - 1],
            {"blk": blk_peer(k)},
        )
        for k in range(1, n_blk)
    ]
    for copy in norm_moves:
        copy.start()
    squares[s] = jnp.broadcast_to(jnp.sum(total * total, axis=1, keepdims=True), squares.shape[1:])
    square_moves = [
        send(
            squares.at[s],
            squares.at[s],
            square_send.at[k - 1],
            square_recv.at[k - 1],
            {"sum": sum_peer(k)},
        )
        for k in range(1, n_sum)
    ]
    for copy in square_moves:
        copy.start()

    def settle(copies, buffer, send_sems, recv_sems):
        for k in range(1, n_blk):
            copies[k - 1].wait_send()
            other = lax.rem(b + n_blk - k, n_blk)
            send(
                buffer.at[other],
                buffer.at[other],
                send_sems.at[k - 1],
                recv_sems.at[k - 1],
                {"blk": blk_peer(k)},
            ).wait_recv()

    lax.fori_loop(turns[1], tiles, turn, 0)
    for k in range(1, n_sum):
        square_moves[k - 1].wait_send()
        other = lax.rem(s + n_sum - k, n_sum)
        send(
            squares.at[other],
            squares.at[other],
            square_send.at[k - 1],
            square_recv.at[k - 1],
            {"sum": sum_peer(k)},
        ).wait_recv()
    inverse[b] = lax.rsqrt(jnp.sum(squares[...], axis=0) / D + 1e-06)
    inverse_moves = [
        send(
            inverse.at[b],
            inverse.at[b],
            inverse_send.at[k - 1],
            inverse_recv.at[k - 1],
            {"blk": blk_peer(k)},
        )
        for k in range(1, n_blk)
    ]
    for copy in inverse_moves:
        copy.start()
    settle(norm_moves, normed, norm_send, norm_recv)
    features = normed[...].astype(jnp.float32).reshape(rows_all, columns).astype(jnp.bfloat16)
    half = rows_all // 2
    to_core = [
        send(
            pre_part.at[1 - core, :, :, spans[c]],
            pre_core.at[:, :, spans[c]],
            core_send.at[c],
            core_recv.at[c],
            {"sum": core_peer},
        )
        for c in range(chunks)
    ]
    to_far = [
        send(
            pre_send.at[:, :, spans[c]],
            pre_far.at[:, :, spans[c]],
            far_send.at[c],
            far_recv.at[c],
            {"sum": far_peer},
        )
        for c in range(chunks)
    ]
    spread = [
        send(
            act.at[core, :, spans[c]],
            act.at[core, :, spans[c]],
            act_send.at[c],
            act_recv.at[c],
            {"sum": core_peer},
        )
        for c in range(chunks)
    ]

    def gate_part(c):
        start = sum(sizes[:c])
        for u in range(start, start + sizes[c], TILE):
            for g in range(2):
                turned = jnp.concatenate(
                    [wg[g, u : u + TILE, f : f + TILE] for f in range(0, columns, TILE)], axis=0
                )
                value = jnp.dot(features, turned, preferred_element_type=jnp.float32)
                value = value.astype(jnp.bfloat16)
                pre_part[0, g, :, u : u + TILE] = value[:half]
                pre_part[1, g, :, u : u + TILE] = value[half:]
        to_core[c].start()

    def core_part(c):
        to_core[c].wait()
        added = pre_part[core, :, :, spans[c]].astype(jnp.float32) + pre_core[
            :, :, spans[c]
        ].astype(jnp.float32)
        pre_sum[:, :, spans[c]] = added
        pre_send[:, :, spans[c]] = added.astype(jnp.bfloat16)
        to_far[c].start()

    def act_part(c):
        if c == 0:
            settle(inverse_moves, inverse, inverse_send, inverse_recv)
        factor = inverse[pl.ds((n_blk // 2) * core, n_blk // 2)].reshape(half, 128)[:, :1]
        to_far[c].wait()
        total = pre_sum[:, :, spans[c]] + pre_far[:, :, spans[c]].astype(jnp.float32)
        gate = total[0] * factor
        up = total[1] * factor
        act[core, :, spans[c]] = (gate / (1.0 + jnp.exp(-gate)) * up).astype(jnp.bfloat16)
        spread[c].start()

    def down_part(c):
        spread[c].wait_send()
        send(
            act.at[1 - core, :, spans[c]],
            act.at[1 - core, :, spans[c]],
            act_send.at[c],
            act_recv.at[c],
            {"sum": core_peer},
        ).wait_recv()
        load_down[c].wait()
        value = jnp.dot(
            act[:, :, spans[c]].reshape(rows_all, sizes[c]),
            wd[spans[c], :],
            preferred_element_type=jnp.float32,
        )
        if c > 0:
            value = value + down_acc[...]
        down_acc[...] = value

    for step in range(chunks + 1):
        if step < chunks:
            gate_part(step)
        if step >= 1:
            core_part(step - 1)
    for step in range(chunks + 1):
        if step < chunks:
            act_part(step)
        if step >= 1:
            down_part(step - 1)
    down_out[...] = down_acc[...].reshape(down_out.shape).astype(jnp.bfloat16)
    moves = [
        send(
            down_out.at[blk_peer(k)],
            down_in.at[k - 1],
            down_send.at[k - 1],
            down_recv.at[k - 1],
            {"blk": blk_peer(k)},
        )
        for k in range(1, n_blk)
    ]
    for copy in moves:
        copy.start()
    total = residual[...] + down_out[b].astype(jnp.float32)
    for k in range(1, n_blk):
        moves[k - 1].wait()
        total = total + down_in[k - 1].astype(jnp.float32)
    out_ref[...] = total


def turn_counts(tiles):
    return [2 * tiles // 5, 18 * tiles // 25]


def chunk_sizes(units):
    tiles = units // TILE
    first, last = 2, 3
    middle = tiles - first - last
    parts = -(-middle // 5)
    sizes = [middle // parts + (i < middle % parts) for i in range(parts)]
    return [TILE * n for n in [first] + sizes + [last]]


def kernel_fits(queries, hidden, out_weight, gate_up_weight):
    n_blk, n_sum = lax.axis_size("blk"), lax.axis_size("sum")
    units, columns = gate_up_weight.shape[1:]
    weights = 2 * (out_weight.size + gate_up_weight.size + units * columns)
    return (
        n_sum == 4
        and n_blk % 2 == 0
        and queries.shape[0] == 2
        and hidden.shape[0] == 8
        and out_weight.shape[0] % (16 * HEAD_SIZE) == 0
        and units % 256 == 0
        and units >= 10 * 256
        and columns % 256 == 0
        and weights <= 53 * 2**20
    )


def layer_in_kernel(
    queries,
    cached_key_rows,
    cached_value_rows,
    incoming_pairs,
    cache_length,
    hidden,
    norm_gain,
    out_weight,
    gate_up_weight,
    down_weight,
):
    n_blk, n_sum = lax.axis_size("blk"), lax.axis_size("sum")
    rows = queries.shape[0]
    own_rows, columns = hidden.shape
    rows_all = n_blk * own_rows
    units = down_weight.shape[0]
    chunks = len(chunk_sizes(units))
    per_block = out_weight.shape[0] // HEAD_SIZE
    bf16, f32 = jnp.bfloat16, jnp.float32
    anywhere = pl.BlockSpec(memory_space=pl.ANY)
    tiles = units // TILE
    sems = [7, tiles, chunks]
    sems += [n_blk * n_sum - 1] * 2 + [n_blk - 1] * 4 + [n_sum - 1] * 2
    sems += [n_blk - 1] * 2 + [chunks] * 6 + [n_blk - 1] * 2
    gain = norm_gain.reshape(columns // 128, 128)
    like = lambda x: pltpu.VMEM(x.shape, x.dtype)
    half = rows_all // 2
    return pl.pallas_call(
        layer_kernel,
        out_shape=pltpu.VMEM(hidden.shape, f32),
        in_specs=[pl.BlockSpec(memory_space=pltpu.SMEM)] + [anywhere] * 9,
        out_specs=pl.BlockSpec(memory_space=pltpu.VMEM),
        scratch_shapes=[
            like(queries),
            like(cached_key_rows),
            like(cached_value_rows),
            like(incoming_pairs),
            like(hidden),
            like(gain),
            like(out_weight),
            like(gate_up_weight),
            like(down_weight),
            pltpu.VMEM((rows, QUERY_HEADS, HEAD_SIZE), f32),
            pltpu.VMEM((rows, n_blk, per_block, HEAD_SIZE), bf16),
            pltpu.VMEM((n_blk, n_sum, rows, per_block, HEAD_SIZE), bf16),
            pltpu.VMEM((rows_all * per_block, HEAD_SIZE), f32),
            pltpu.VMEM((n_blk, own_rows, columns), bf16),
            pltpu.VMEM((n_blk - 1, own_rows, columns), bf16),
            pltpu.VMEM(hidden.shape, f32),
            pltpu.VMEM((n_blk, own_rows, columns), bf16),
            pltpu.VMEM((n_sum, own_rows, 128), f32),
            pltpu.VMEM((n_blk, own_rows, 128), f32),
            pltpu.VMEM((2, 2, half, units), bf16),
            pltpu.VMEM((2, half, units), bf16),
            pltpu.VMEM((2, half, units), f32),
            pltpu.VMEM((2, half, units), bf16),
            pltpu.VMEM((2, half, units), bf16),
            pltpu.VMEM((2, half, units), bf16),
            pltpu.VMEM((rows_all, columns), f32),
            pltpu.VMEM((n_blk, own_rows, columns), bf16),
            pltpu.VMEM((n_blk - 1, own_rows, columns), bf16),
        ]
        + [pltpu.SemaphoreType.DMA((n,)) for n in sems],
        compiler_params=pltpu.CompilerParams(
            collective_id=0, has_side_effects=True, vmem_limit_bytes=60 * 2**20
        ),
    )(
        cache_length,
        queries,
        cached_key_rows,
        cached_value_rows,
        incoming_pairs,
        hidden,
        gain,
        out_weight,
        gate_up_weight,
        down_weight,
    )


def on_device(
    queries,
    cached_key_rows,
    cached_value_rows,
    incoming_pairs,
    cache_length,
    hidden,
    norm_gain,
    out_weight,
    gate_up_weight,
    down_weight,
):
    if kernel_fits(queries, hidden, out_weight, gate_up_weight):
        return layer_in_kernel(
            queries,
            cached_key_rows,
            cached_value_rows,
            incoming_pairs,
            cache_length,
            hidden,
            norm_gain,
            out_weight,
            gate_up_weight,
            down_weight,
        )
    attended = attend_padded(
        queries, cached_key_rows, cached_value_rows, incoming_pairs, cache_length
    )
    spread = lax.all_to_all(attended, "blk", split_axis=1, concat_axis=0, tiled=True)
    spread = spread.reshape(lax.axis_size("blk"), attended.shape[0], spread.shape[1])
    heads_rows = lax.all_gather(spread, "sum", axis=1, tiled=True).reshape(-1, spread.shape[2])
    picked = heads_rows
    projected = lax.psum_scatter(
        jnp.dot(picked, out_weight, preferred_element_type=jnp.float32).astype(jnp.bfloat16),
        "blk",
        scatter_dimension=0,
        tiled=True,
    ).astype(jnp.float32)
    residual = hidden + projected
    square_sum = lax.psum(jnp.sum(residual * residual, axis=1), "sum")
    inverse = lax.rsqrt(square_sum / D + 1e-06)
    normed = (residual * inverse[:, None] * norm_gain[None, :]).astype(jnp.bfloat16)
    pre_terms = jnp.einsum(
        "nd,gfd->ngf",
        lax.all_gather(normed, "blk", axis=0, tiled=True),
        gate_up_weight,
        preferred_element_type=jnp.float32,
    )
    summed = lax.psum(pre_terms.astype(jnp.bfloat16), "sum").astype(jnp.float32)
    activated = (jax.nn.silu(summed[:, 0]) * summed[:, 1]).astype(jnp.bfloat16)
    picked = activated
    feed_sum = lax.psum_scatter(
        jnp.dot(picked, down_weight, preferred_element_type=jnp.float32).astype(jnp.bfloat16),
        "blk",
        scatter_dimension=0,
        tiled=True,
    ).astype(jnp.float32)
    return residual + feed_sum


def solution(mesh):
    placed = (
        P(("groups", "blk", "sum"), None),
        P(("groups", "blk", "sum"), None, None),
        P(("groups", "blk", "sum"), None, None),
        P(("groups", "blk", "sum"), None, None),
        P(("groups", "blk", "sum")),
        P(("groups", "blk"), "sum"),
        P("sum"),
        P("blk", "sum"),
        P(None, "blk", "sum"),
        P("blk", "sum"),
    )
    return jax.shard_map(
        on_device,
        mesh=mesh,
        in_specs=placed,
        out_specs=P(("groups", "blk"), "sum"),
        check_vma=False,
    )
```

```python
import jax
import jax.numpy as jnp
from jax import lax
from jax.experimental import pallas as pl
from jax.experimental.pallas import tpu as pltpu
from jax.sharding import PartitionSpec as P

D = 5120
QUERY_HEADS = 64
KEY_VALUE_HEADS = 8
HEAD_SIZE = 128
CACHE_SLOTS = 128


def attend_padded(queries, cached_key_rows, cached_value_rows, incoming_pairs, cache_length):
    count_of_rows = queries.shape[0]
    score_scale = HEAD_SIZE ** (-0.5)
    query_head_count = queries.reshape(
        count_of_rows, KEY_VALUE_HEADS, QUERY_HEADS // KEY_VALUE_HEADS, HEAD_SIZE
    )
    key_head_count = cached_key_rows.reshape(count_of_rows, CACHE_SLOTS, KEY_VALUE_HEADS, HEAD_SIZE)
    value_head_count = cached_value_rows.reshape(
        count_of_rows, CACHE_SLOTS, KEY_VALUE_HEADS, HEAD_SIZE
    )
    incoming_key = incoming_pairs[:, 0].reshape(count_of_rows, KEY_VALUE_HEADS, HEAD_SIZE)
    incoming_value = incoming_pairs[:, 1].reshape(count_of_rows, KEY_VALUE_HEADS, HEAD_SIZE)
    scores = (
        jnp.einsum(
            "nkgd,nlkd->nkgl", query_head_count, key_head_count, preferred_element_type=jnp.float32
        )
        * score_scale
    )
    own_score = (
        jnp.einsum(
            "nkgd,nkd->nkg", query_head_count, incoming_key, preferred_element_type=jnp.float32
        )
        * score_scale
    )
    live_mask = jnp.arange(CACHE_SLOTS)[None, :] < cache_length[:, None]
    scores = jnp.where(live_mask[:, None, None, :], scores, -jnp.inf)
    row_max = jnp.maximum(jnp.max(scores, axis=-1), own_score)
    cache_terms = jnp.exp(scores - row_max[..., None])
    own_term = jnp.exp(own_score - row_max)
    row_total = jnp.sum(cache_terms, axis=-1) + own_term
    weights = (cache_terms / row_total[..., None]).astype(jnp.bfloat16)
    own_weight = (own_term / row_total).astype(jnp.bfloat16)
    mixed = jnp.einsum(
        "nkgl,nlkd->nkgd", weights, value_head_count, preferred_element_type=jnp.float32
    )
    mixed = (
        mixed
        + own_weight.astype(jnp.float32)[..., None]
        * incoming_value.astype(jnp.float32)[:, :, None, :]
    )
    return mixed.astype(jnp.bfloat16).reshape(count_of_rows, QUERY_HEADS * HEAD_SIZE)


MESH = pl.DeviceIdType.MESH


TILE = 256
WO_PIECES = 8
WO_AT = 0


def layer_kernel(
    lengths,
    q_hbm,
    k_hbm,
    v_hbm,
    pair_hbm,
    hidden_hbm,
    gain_hbm,
    wo_hbm,
    wg_hbm,
    wd_hbm,
    out_ref,
    q_buf,
    k_buf,
    v_buf,
    pair_buf,
    hidden_buf,
    gain_buf,
    wo,
    wg,
    wd,
    q_rows,
    mixed,
    heads_all,
    heads_f32,
    proj_out,
    proj_in,
    residual,
    normed,
    squares,
    inverse,
    pre_part,
    pre_core,
    pre_sum,
    pre_send,
    pre_far,
    act,
    down_acc,
    down_out,
    down_in,
    load_sem,
    wo_sem,
    wg_sem,
    wd_sem,
    heads_send,
    heads_recv,
    proj_send,
    proj_recv,
    norm_send,
    norm_recv,
    square_send,
    square_recv,
    inverse_send,
    inverse_recv,
    core_send,
    core_recv,
    far_send,
    far_recv,
    act_send,
    act_recv,
    down_send,
    down_recv,
):
    n_blk, n_sum = lax.axis_size("blk"), lax.axis_size("sum")
    rows_here = q_buf.shape[0]
    units, columns = wd.shape
    tiles = units // TILE
    sizes = chunk_sizes(units)
    chunks = len(sizes)
    spans = [pl.ds(sum(sizes[:c]), sizes[c]) for c in range(chunks)]
    b, s = lax.axis_index("blk"), lax.axis_index("sum")
    core = lax.rem(s, 2)
    core_peer = s + 1 - 2 * core
    far_peer = lax.rem(s + 2, n_sum)

    def blk_peer(k):
        return lax.rem(b + k, n_blk)

    def sum_peer(k):
        return lax.rem(s + k, n_sum)

    def send(src, dst, send_sem, recv_sem, where):
        return pltpu.make_async_remote_copy(
            src_ref=src,
            dst_ref=dst,
            send_sem=send_sem,
            recv_sem=recv_sem,
            device_id=where,
            device_id_type=MESH,
        )

    blk_order = [n_blk // 2] + [k for k in range(1, n_blk) if k != n_blk // 2]
    peers = [(i, j) for i in blk_order + [0] for j in (2, 3, 1, 0) if (i, j) != (0, 0)]

    barrier = pltpu.get_barrier_semaphore()
    first = [
        pltpu.make_async_copy(src, dst, load_sem.at[i])
        for i, (src, dst) in enumerate(
            [
                (q_hbm, q_buf),
                (k_hbm, k_buf),
                (pair_hbm, pair_buf),
                (v_hbm, v_buf),
                (hidden_hbm, hidden_buf),
                (gain_hbm, gain_buf),
            ]
        )
    ]

    def load_gate(t):
        span = pl.ds(pl.multiple_of(t * TILE, TILE), TILE)
        return pltpu.make_async_copy(wg_hbm.at[:, span, :], wg.at[:, span, :], wg_sem.at[t])

    def load_down(t):
        span = pl.ds(pl.multiple_of(t * TILE, TILE), TILE)
        return pltpu.make_async_copy(wd_hbm.at[span, :], wd.at[span, :], wd_sem.at[t])

    piece = wo.shape[0] // WO_PIECES
    load_out = [
        pltpu.make_async_copy(
            wo_hbm.at[pl.ds(i * piece, piece), :], wo.at[pl.ds(i * piece, piece), :], wo_sem.at[i]
        )
        for i in range(WO_PIECES)
    ]
    for copy in first[:4]:
        copy.start()
    for i, j in peers:
        pl.semaphore_signal(
            barrier,
            inc=1,
            device_id={"blk": blk_peer(i), "sum": sum_peer(j)},
            device_id_type=MESH,
        )
    first[0].wait()
    for copy in load_out + first[4:]:
        copy.start()
    for copy in first[1:4]:
        copy.wait()
    turns = turn_counts(tiles)

    def start_gate(t, carry):
        load_gate(t).start()
        return carry

    def start_down(t, carry):
        load_down(t).start()
        return carry

    lax.fori_loop(0, tiles, start_gate, 0)
    lax.fori_loop(0, tiles, start_down, 0)

    group = QUERY_HEADS // KEY_VALUE_HEADS
    queries = q_buf[...].astype(jnp.float32)
    for r in range(rows_here):
        for h in range(QUERY_HEADS):
            q_rows[r, h : h + 1, :] = queries[r : r + 1, h * HEAD_SIZE : (h + 1) * HEAD_SIZE]
    score_scale = HEAD_SIZE ** (-0.5)
    staged = []
    for r in range(rows_here):
        q32 = q_rows[r]
        q16 = q32.astype(jnp.bfloat16)
        new_key = pair_buf[r, 0:1, :].astype(jnp.float32)
        new_value = pair_buf[r, 1:2, :].astype(jnp.float32)
        scores, keys_new, values_new = [], [], []
        for j in range(KEY_VALUE_HEADS):
            cols = slice(j * HEAD_SIZE, (j + 1) * HEAD_SIZE)
            scores.append(
                lax.dot_general(
                    q16[j * group : (j + 1) * group],
                    k_buf[r, :, cols],
                    (((1,), (1,)), ((), ())),
                    preferred_element_type=jnp.float32,
                )
            )
            keys_new.append(jnp.broadcast_to(new_key[:, cols], (group, HEAD_SIZE)))
            values_new.append(jnp.broadcast_to(new_value[:, cols], (group, HEAD_SIZE)))
        scores = jnp.concatenate(scores, axis=0) * score_scale
        own = jnp.sum(q32 * jnp.concatenate(keys_new, axis=0), axis=1, keepdims=True) * score_scale
        staged.append((scores, own, jnp.concatenate(values_new, axis=0)))
    weighted = []
    for r in range(rows_here):
        scores, own, _ = staged[r]
        position = lax.broadcasted_iota(jnp.int32, scores.shape, 1)
        scores = jnp.where(position < lengths[r], scores, -jnp.inf)
        row_max = jnp.maximum(jnp.max(scores, axis=1, keepdims=True), own)
        terms = jnp.exp(scores - row_max)
        own_term = jnp.exp(own - row_max)
        total = jnp.sum(terms, axis=1, keepdims=True) + own_term
        weights = (terms / total).astype(jnp.bfloat16)
        weighted.append((weights, (own_term / total).astype(jnp.bfloat16).astype(jnp.float32)))
    for r in range(rows_here):
        weights, own_weight = weighted[r]
        outs = []
        for j in range(KEY_VALUE_HEADS):
            cols = slice(j * HEAD_SIZE, (j + 1) * HEAD_SIZE)
            outs.append(
                jnp.dot(
                    weights[j * group : (j + 1) * group],
                    v_buf[r, :, cols],
                    preferred_element_type=jnp.float32,
                )
            )
        result = jnp.concatenate(outs, axis=0) + own_weight * staged[r][2]
        mixed[r] = result.astype(jnp.bfloat16).reshape(mixed.shape[1:])

    pl.semaphore_wait(barrier, len(peers))
    moves = []
    for n, (i, j) in enumerate(peers):
        moves.append(
            send(
                mixed.at[:, blk_peer(i)],
                heads_all.at[b, s],
                heads_send.at[n],
                heads_recv.at[n],
                {"blk": blk_peer(i), "sum": sum_peer(j)},
            )
        )
    for copy in moves:
        copy.start()
    heads_all[b, s] = mixed[:, b]

    def turn(t, carry):
        load_gate(t).wait()
        span = pl.ds(pl.multiple_of(t * TILE, TILE), TILE)
        for g in range(2):
            for f in range(columns // TILE):
                cols = slice(f * TILE, (f + 1) * TILE)
                wg[g, span, cols] = wg[g, span, cols].T
        return carry

    lax.fori_loop(0, turns[0], turn, 0)
    for n, (i, j) in enumerate(peers):
        moves[n].wait_send()
        other_b, other_s = lax.rem(b + n_blk - i, n_blk), lax.rem(s + n_sum - j, n_sum)
        send(
            mixed.at[:, blk_peer(i)],
            heads_all.at[other_b, other_s],
            heads_send.at[n],
            heads_recv.at[n],
            {"blk": blk_peer(i), "sum": sum_peer(j)},
        ).wait_recv()
    heads_f32[...] = heads_all[...].astype(jnp.float32).reshape(heads_f32.shape)
    per_block = wo.shape[0] // HEAD_SIZE
    rows_all = n_blk * n_sum * rows_here
    picked = jnp.concatenate(
        [
            heads_f32[pl.ds(h, rows_all, stride=per_block), :].astype(jnp.bfloat16)
            for h in range(per_block)
        ],
        axis=1,
    )
    for copy in load_out:
        copy.wait()
    projected = jnp.dot(picked, wo[...], preferred_element_type=jnp.float32)
    proj_out[...] = projected.reshape(proj_out.shape).astype(jnp.bfloat16)
    moves = [
        send(
            proj_out.at[blk_peer(k)],
            proj_in.at[k - 1],
            proj_send.at[k - 1],
            proj_recv.at[k - 1],
            {"blk": blk_peer(k)},
        )
        for k in range(1, n_blk)
    ]
    for copy in moves:
        copy.start()
    lax.fori_loop(turns[0], turns[1], turn, 0)
    first[4].wait()
    first[5].wait()
    total = hidden_buf[...] + proj_out[b].astype(jnp.float32)
    for k in range(1, n_blk):
        moves[k - 1].wait()
        total = total + proj_in[k - 1].astype(jnp.float32)
    residual[...] = total
    scaled = [
        total[:, n * 128 : (n + 1) * 128] * gain_buf[n : n + 1, :] for n in range(columns // 128)
    ]
    normed[b] = jnp.concatenate(scaled, axis=1).astype(jnp.bfloat16)
    norm_moves = [
        send(
            normed.at[b],
            normed.at[b],
            norm_send.at[k - 1],
            norm_recv.at[k - 1],
            {"blk": blk_peer(k)},
        )
        for k in range(1, n_blk)
    ]
    for copy in norm_moves:
        copy.start()
    squares[s] = jnp.broadcast_to(jnp.sum(total * total, axis=1, keepdims=True), squares.shape[1:])
    square_moves = [
        send(
            squares.at[s],
            squares.at[s],
            square_send.at[k - 1],
            square_recv.at[k - 1],
            {"sum": sum_peer(k)},
        )
        for k in range(1, n_sum)
    ]
    for copy in square_moves:
        copy.start()

    def settle(copies, buffer, send_sems, recv_sems):
        for k in range(1, n_blk):
            copies[k - 1].wait_send()
            other = lax.rem(b + n_blk - k, n_blk)
            send(
                buffer.at[other],
                buffer.at[other],
                send_sems.at[k - 1],
                recv_sems.at[k - 1],
                {"blk": blk_peer(k)},
            ).wait_recv()

    lax.fori_loop(turns[1], tiles, turn, 0)
    for k in range(1, n_sum):
        square_moves[k - 1].wait_send()
        other = lax.rem(s + n_sum - k, n_sum)
        send(
            squares.at[other],
            squares.at[other],
            square_send.at[k - 1],
            square_recv.at[k - 1],
            {"sum": sum_peer(k)},
        ).wait_recv()
    inverse[b] = lax.rsqrt(jnp.sum(squares[...], axis=0) / D + 1e-06)
    inverse_moves = [
        send(
            inverse.at[b],
            inverse.at[b],
            inverse_send.at[k - 1],
            inverse_recv.at[k - 1],
            {"blk": blk_peer(k)},
        )
        for k in range(1, n_blk)
    ]
    for copy in inverse_moves:
        copy.start()
    settle(norm_moves, normed, norm_send, norm_recv)
    features = normed[...].astype(jnp.float32).reshape(rows_all, columns).astype(jnp.bfloat16)
    half = rows_all // 2
    to_core = [
        send(
            pre_part.at[1 - core, :, :, spans[c]],
            pre_core.at[:, :, spans[c]],
            core_send.at[c],
            core_recv.at[c],
            {"sum": core_peer},
        )
        for c in range(chunks)
    ]
    to_far = [
        send(
            pre_send.at[:, :, spans[c]],
            pre_far.at[:, :, spans[c]],
            far_send.at[c],
            far_recv.at[c],
            {"sum": far_peer},
        )
        for c in range(chunks)
    ]
    spread = [
        send(
            act.at[core, :, spans[c]],
            act.at[core, :, spans[c]],
            act_send.at[c],
            act_recv.at[c],
            {"sum": core_peer},
        )
        for c in range(chunks)
    ]

    def gate_part(c):
        start = sum(sizes[:c])
        for u in range(start, start + sizes[c], TILE):
            for g in range(2):
                turned = jnp.concatenate(
                    [wg[g, u : u + TILE, f : f + TILE] for f in range(0, columns, TILE)], axis=0
                )
                value = jnp.dot(features, turned, preferred_element_type=jnp.float32)
                value = value.astype(jnp.bfloat16)
                pre_part[0, g, :, u : u + TILE] = value[:half]
                pre_part[1, g, :, u : u + TILE] = value[half:]
        to_core[c].start()

    def core_part(c):
        to_core[c].wait()
        added = pre_part[core, :, :, spans[c]].astype(jnp.float32) + pre_core[
            :, :, spans[c]
        ].astype(jnp.float32)
        pre_sum[:, :, spans[c]] = added
        pre_send[:, :, spans[c]] = added.astype(jnp.bfloat16)
        to_far[c].start()

    def act_part(c):
        if c == 0:
            settle(inverse_moves, inverse, inverse_send, inverse_recv)
        factor = inverse[pl.ds((n_blk // 2) * core, n_blk // 2)].reshape(half, 128)[:, :1]
        to_far[c].wait()
        total = pre_sum[:, :, spans[c]] + pre_far[:, :, spans[c]].astype(jnp.float32)
        gate = total[0] * factor
        up = total[1] * factor
        act[core, :, spans[c]] = (gate / (1.0 + jnp.exp(-gate)) * up).astype(jnp.bfloat16)
        spread[c].start()

    def down_part(c):
        spread[c].wait_send()
        send(
            act.at[1 - core, :, spans[c]],
            act.at[1 - core, :, spans[c]],
            act_send.at[c],
            act_recv.at[c],
            {"sum": core_peer},
        ).wait_recv()
        for t in range(sum(sizes[:c]) // TILE, sum(sizes[: c + 1]) // TILE):
            load_down(t).wait()
        value = jnp.dot(
            act[:, :, spans[c]].reshape(rows_all, sizes[c]),
            wd[spans[c], :],
            preferred_element_type=jnp.float32,
        )
        if c > 0:
            value = value + down_acc[...]
        down_acc[...] = value

    for step in range(chunks + 1):
        if step < chunks:
            gate_part(step)
        if step >= 1:
            core_part(step - 1)
    for step in range(chunks + 1):
        if step < chunks:
            act_part(step)
        if step >= 1:
            down_part(step - 1)
    down_out[...] = down_acc[...].reshape(down_out.shape).astype(jnp.bfloat16)
    moves = [
        send(
            down_out.at[blk_peer(k)],
            down_in.at[k - 1],
            down_send.at[k - 1],
            down_recv.at[k - 1],
            {"blk": blk_peer(k)},
        )
        for k in range(1, n_blk)
    ]
    for copy in moves:
        copy.start()
    total = residual[...] + down_out[b].astype(jnp.float32)
    for k in range(1, n_blk):
        moves[k - 1].wait()
        total = total + down_in[k - 1].astype(jnp.float32)
    out_ref[...] = total


def turn_counts(tiles):
    return [2 * tiles // 5, 18 * tiles // 25]


def chunk_sizes(units):
    tiles = units // TILE
    first, last = 2, 3
    middle = tiles - first - last
    parts = -(-middle // 5)
    sizes = [middle // parts + (i < middle % parts) for i in range(parts)]
    return [TILE * n for n in [first] + sizes + [last]]


def kernel_fits(queries, hidden, out_weight, gate_up_weight):
    n_blk, n_sum = lax.axis_size("blk"), lax.axis_size("sum")
    units, columns = gate_up_weight.shape[1:]
    weights = 2 * (out_weight.size + gate_up_weight.size + units * columns)
    return (
        n_sum == 4
        and n_blk % 2 == 0
        and queries.shape[0] == 2
        and hidden.shape[0] == 8
        and out_weight.shape[0] % (16 * HEAD_SIZE) == 0
        and units % 256 == 0
        and units >= 10 * 256
        and columns % 256 == 0
        and weights <= 53 * 2**20
    )


def layer_in_kernel(
    queries,
    cached_key_rows,
    cached_value_rows,
    incoming_pairs,
    cache_length,
    hidden,
    norm_gain,
    out_weight,
    gate_up_weight,
    down_weight,
):
    n_blk, n_sum = lax.axis_size("blk"), lax.axis_size("sum")
    rows = queries.shape[0]
    own_rows, columns = hidden.shape
    rows_all = n_blk * own_rows
    units = down_weight.shape[0]
    chunks = len(chunk_sizes(units))
    per_block = out_weight.shape[0] // HEAD_SIZE
    bf16, f32 = jnp.bfloat16, jnp.float32
    anywhere = pl.BlockSpec(memory_space=pl.ANY)
    tiles = units // TILE
    sems = [6, WO_PIECES, tiles, tiles]
    sems += [n_blk * n_sum - 1] * 2 + [n_blk - 1] * 4 + [n_sum - 1] * 2
    sems += [n_blk - 1] * 2 + [chunks] * 6 + [n_blk - 1] * 2
    gain = norm_gain.reshape(columns // 128, 128)
    like = lambda x: pltpu.VMEM(x.shape, x.dtype)
    half = rows_all // 2
    return pl.pallas_call(
        layer_kernel,
        out_shape=pltpu.VMEM(hidden.shape, f32),
        in_specs=[pl.BlockSpec(memory_space=pltpu.SMEM)] + [anywhere] * 9,
        out_specs=pl.BlockSpec(memory_space=pltpu.VMEM),
        scratch_shapes=[
            like(queries),
            like(cached_key_rows),
            like(cached_value_rows),
            like(incoming_pairs),
            like(hidden),
            like(gain),
            like(out_weight),
            like(gate_up_weight),
            like(down_weight),
            pltpu.VMEM((rows, QUERY_HEADS, HEAD_SIZE), f32),
            pltpu.VMEM((rows, n_blk, per_block, HEAD_SIZE), bf16),
            pltpu.VMEM((n_blk, n_sum, rows, per_block, HEAD_SIZE), bf16),
            pltpu.VMEM((rows_all * per_block, HEAD_SIZE), f32),
            pltpu.VMEM((n_blk, own_rows, columns), bf16),
            pltpu.VMEM((n_blk - 1, own_rows, columns), bf16),
            pltpu.VMEM(hidden.shape, f32),
            pltpu.VMEM((n_blk, own_rows, columns), bf16),
            pltpu.VMEM((n_sum, own_rows, 128), f32),
            pltpu.VMEM((n_blk, own_rows, 128), f32),
            pltpu.VMEM((2, 2, half, units), bf16),
            pltpu.VMEM((2, half, units), bf16),
            pltpu.VMEM((2, half, units), f32),
            pltpu.VMEM((2, half, units), bf16),
            pltpu.VMEM((2, half, units), bf16),
            pltpu.VMEM((2, half, units), bf16),
            pltpu.VMEM((rows_all, columns), f32),
            pltpu.VMEM((n_blk, own_rows, columns), bf16),
            pltpu.VMEM((n_blk - 1, own_rows, columns), bf16),
        ]
        + [pltpu.SemaphoreType.DMA((n,)) for n in sems],
        compiler_params=pltpu.CompilerParams(
            collective_id=0, has_side_effects=True, vmem_limit_bytes=60 * 2**20
        ),
    )(
        cache_length,
        queries,
        cached_key_rows,
        cached_value_rows,
        incoming_pairs,
        hidden,
        gain,
        out_weight,
        gate_up_weight,
        down_weight,
    )


def on_device(
    queries,
    cached_key_rows,
    cached_value_rows,
    incoming_pairs,
    cache_length,
    hidden,
    norm_gain,
    out_weight,
    gate_up_weight,
    down_weight,
):
    if kernel_fits(queries, hidden, out_weight, gate_up_weight):
        return layer_in_kernel(
            queries,
            cached_key_rows,
            cached_value_rows,
            incoming_pairs,
            cache_length,
            hidden,
            norm_gain,
            out_weight,
            gate_up_weight,
            down_weight,
        )
    attended = attend_padded(
        queries, cached_key_rows, cached_value_rows, incoming_pairs, cache_length
    )
    spread = lax.all_to_all(attended, "blk", split_axis=1, concat_axis=0, tiled=True)
    spread = spread.reshape(lax.axis_size("blk"), attended.shape[0], spread.shape[1])
    heads_rows = lax.all_gather(spread, "sum", axis=1, tiled=True).reshape(-1, spread.shape[2])
    picked = heads_rows
    projected = lax.psum_scatter(
        jnp.dot(picked, out_weight, preferred_element_type=jnp.float32).astype(jnp.bfloat16),
        "blk",
        scatter_dimension=0,
        tiled=True,
    ).astype(jnp.float32)
    residual = hidden + projected
    square_sum = lax.psum(jnp.sum(residual * residual, axis=1), "sum")
    inverse = lax.rsqrt(square_sum / D + 1e-06)
    normed = (residual * inverse[:, None] * norm_gain[None, :]).astype(jnp.bfloat16)
    pre_terms = jnp.einsum(
        "nd,gfd->ngf",
        lax.all_gather(normed, "blk", axis=0, tiled=True),
        gate_up_weight,
        preferred_element_type=jnp.float32,
    )
    summed = lax.psum(pre_terms.astype(jnp.bfloat16), "sum").astype(jnp.float32)
    activated = (jax.nn.silu(summed[:, 0]) * summed[:, 1]).astype(jnp.bfloat16)
    picked = activated
    feed_sum = lax.psum_scatter(
        jnp.dot(picked, down_weight, preferred_element_type=jnp.float32).astype(jnp.bfloat16),
        "blk",
        scatter_dimension=0,
        tiled=True,
    ).astype(jnp.float32)
    return residual + feed_sum


def solution(mesh):
    placed = (
        P(("groups", "blk", "sum"), None),
        P(("groups", "blk", "sum"), None, None),
        P(("groups", "blk", "sum"), None, None),
        P(("groups", "blk", "sum"), None, None),
        P(("groups", "blk", "sum")),
        P(("groups", "blk"), "sum"),
        P("sum"),
        P("blk", "sum"),
        P(None, "blk", "sum"),
        P("blk", "sum"),
    )
    return jax.shard_map(
        on_device,
        mesh=mesh,
        in_specs=placed,
        out_specs=P(("groups", "blk"), "sum"),
        check_vma=False,
    )
```

```python
import jax
import jax.numpy as jnp
from jax import lax
from jax.experimental import pallas as pl
from jax.experimental.pallas import tpu as pltpu
from jax.sharding import PartitionSpec as P

D = 5120
QUERY_HEADS = 64
KEY_VALUE_HEADS = 8
HEAD_SIZE = 128
CACHE_SLOTS = 128


def attend_padded(queries, cached_key_rows, cached_value_rows, incoming_pairs, cache_length):
    count_of_rows = queries.shape[0]
    score_scale = HEAD_SIZE ** (-0.5)
    query_head_count = queries.reshape(
        count_of_rows, KEY_VALUE_HEADS, QUERY_HEADS // KEY_VALUE_HEADS, HEAD_SIZE
    )
    key_head_count = cached_key_rows.reshape(count_of_rows, CACHE_SLOTS, KEY_VALUE_HEADS, HEAD_SIZE)
    value_head_count = cached_value_rows.reshape(
        count_of_rows, CACHE_SLOTS, KEY_VALUE_HEADS, HEAD_SIZE
    )
    incoming_key = incoming_pairs[:, 0].reshape(count_of_rows, KEY_VALUE_HEADS, HEAD_SIZE)
    incoming_value = incoming_pairs[:, 1].reshape(count_of_rows, KEY_VALUE_HEADS, HEAD_SIZE)
    scores = (
        jnp.einsum(
            "nkgd,nlkd->nkgl", query_head_count, key_head_count, preferred_element_type=jnp.float32
        )
        * score_scale
    )
    own_score = (
        jnp.einsum(
            "nkgd,nkd->nkg", query_head_count, incoming_key, preferred_element_type=jnp.float32
        )
        * score_scale
    )
    live_mask = jnp.arange(CACHE_SLOTS)[None, :] < cache_length[:, None]
    scores = jnp.where(live_mask[:, None, None, :], scores, -jnp.inf)
    row_max = jnp.maximum(jnp.max(scores, axis=-1), own_score)
    cache_terms = jnp.exp(scores - row_max[..., None])
    own_term = jnp.exp(own_score - row_max)
    row_total = jnp.sum(cache_terms, axis=-1) + own_term
    weights = (cache_terms / row_total[..., None]).astype(jnp.bfloat16)
    own_weight = (own_term / row_total).astype(jnp.bfloat16)
    mixed = jnp.einsum(
        "nkgl,nlkd->nkgd", weights, value_head_count, preferred_element_type=jnp.float32
    )
    mixed = (
        mixed
        + own_weight.astype(jnp.float32)[..., None]
        * incoming_value.astype(jnp.float32)[:, :, None, :]
    )
    return mixed.astype(jnp.bfloat16).reshape(count_of_rows, QUERY_HEADS * HEAD_SIZE)


MESH = pl.DeviceIdType.MESH


TILE = 256
WO_PIECES = 8
DOWN_LAG = 1


def layer_kernel(
    lengths,
    q_hbm,
    k_hbm,
    v_hbm,
    pair_hbm,
    hidden_hbm,
    gain_hbm,
    wo_hbm,
    wg_hbm,
    wd_hbm,
    out_ref,
    q_buf,
    k_buf,
    v_buf,
    pair_buf,
    hidden_buf,
    gain_buf,
    wo,
    wg,
    wd,
    q_rows,
    mixed,
    heads_all,
    heads_f32,
    proj_out,
    proj_in,
    residual,
    normed,
    squares,
    inverse,
    pre_part,
    pre_core,
    pre_sum,
    pre_send,
    pre_far,
    act,
    down_acc,
    down_out,
    down_in,
    load_sem,
    wo_sem,
    wg_sem,
    wd_sem,
    heads_send,
    heads_recv,
    proj_send,
    proj_recv,
    norm_send,
    norm_recv,
    square_send,
    square_recv,
    inverse_send,
    inverse_recv,
    core_send,
    core_recv,
    far_send,
    far_recv,
    act_send,
    act_recv,
    down_send,
    down_recv,
):
    n_blk, n_sum = lax.axis_size("blk"), lax.axis_size("sum")
    rows_here = q_buf.shape[0]
    units, columns = wd.shape
    tiles = units // TILE
    sizes = chunk_sizes(units)
    chunks = len(sizes)
    ends = [sum(sizes[: c + 1]) for c in range(chunks)]
    spans = [pl.ds(ends[c] - sizes[c], sizes[c]) for c in range(chunks)]
    b, s = lax.axis_index("blk"), lax.axis_index("sum")
    core = lax.rem(s, 2)
    core_peer = s + 1 - 2 * core
    far_peer = lax.rem(s + 2, n_sum)

    def blk_peer(k):
        return lax.rem(b + k, n_blk)

    def sum_peer(k):
        return lax.rem(s + k, n_sum)

    def send(src, dst, send_sem, recv_sem, where):
        return pltpu.make_async_remote_copy(
            src_ref=src,
            dst_ref=dst,
            send_sem=send_sem,
            recv_sem=recv_sem,
            device_id=where,
            device_id_type=MESH,
        )

    blk_order = [n_blk // 2] + [k for k in range(1, n_blk) if k != n_blk // 2]
    peers = [(i, j) for i in blk_order + [0] for j in (2, 3, 1, 0) if (i, j) != (0, 0)]

    barrier = pltpu.get_barrier_semaphore()
    first = [
        pltpu.make_async_copy(src, dst, load_sem.at[i])
        for i, (src, dst) in enumerate(
            [
                (q_hbm, q_buf),
                (k_hbm, k_buf),
                (pair_hbm, pair_buf),
                (v_hbm, v_buf),
                (hidden_hbm, hidden_buf),
                (gain_hbm, gain_buf),
            ]
        )
    ]

    def load_gate(t):
        span = pl.ds(pl.multiple_of(t * TILE, TILE), TILE)
        return pltpu.make_async_copy(wg_hbm.at[:, span, :], wg.at[:, span, :], wg_sem.at[t])

    def load_down(t):
        span = pl.ds(pl.multiple_of(t * TILE, TILE), TILE)
        return pltpu.make_async_copy(wd_hbm.at[span, :], wd.at[span, :], wd_sem.at[t])

    piece = wo.shape[0] // WO_PIECES
    load_out = [
        pltpu.make_async_copy(
            wo_hbm.at[pl.ds(i * piece, piece), :], wo.at[pl.ds(i * piece, piece), :], wo_sem.at[i]
        )
        for i in range(WO_PIECES)
    ]
    for copy in first[:4]:
        copy.start()
    for i, j in peers:
        pl.semaphore_signal(
            barrier,
            inc=1,
            device_id={"blk": blk_peer(i), "sum": sum_peer(j)},
            device_id_type=MESH,
        )
    first[0].wait()
    for copy in load_out + first[4:]:
        copy.start()
    for copy in first[1:4]:
        copy.wait()
    turns = turn_counts(tiles)

    def start_gate(t, carry):
        load_gate(t).start()
        return carry

    def start_down(t, carry):
        load_down(t).start()
        return carry

    lax.fori_loop(0, tiles, start_gate, 0)
    lax.fori_loop(0, tiles, start_down, 0)

    group = QUERY_HEADS // KEY_VALUE_HEADS
    queries = q_buf[...].astype(jnp.float32)
    for r in range(rows_here):
        for h in range(QUERY_HEADS):
            q_rows[r, h : h + 1, :] = queries[r : r + 1, h * HEAD_SIZE : (h + 1) * HEAD_SIZE]
    score_scale = HEAD_SIZE ** (-0.5)
    staged = []
    for r in range(rows_here):
        q32 = q_rows[r]
        q16 = q32.astype(jnp.bfloat16)
        new_key = pair_buf[r, 0:1, :].astype(jnp.float32)
        new_value = pair_buf[r, 1:2, :].astype(jnp.float32)
        scores, keys_new, values_new = [], [], []
        for j in range(KEY_VALUE_HEADS):
            cols = slice(j * HEAD_SIZE, (j + 1) * HEAD_SIZE)
            scores.append(
                lax.dot_general(
                    q16[j * group : (j + 1) * group],
                    k_buf[r, :, cols],
                    (((1,), (1,)), ((), ())),
                    preferred_element_type=jnp.float32,
                )
            )
            keys_new.append(jnp.broadcast_to(new_key[:, cols], (group, HEAD_SIZE)))
            values_new.append(jnp.broadcast_to(new_value[:, cols], (group, HEAD_SIZE)))
        scores = jnp.concatenate(scores, axis=0) * score_scale
        own = jnp.sum(q32 * jnp.concatenate(keys_new, axis=0), axis=1, keepdims=True) * score_scale
        staged.append((scores, own, jnp.concatenate(values_new, axis=0)))
    weighted = []
    for r in range(rows_here):
        scores, own, _ = staged[r]
        position = lax.broadcasted_iota(jnp.int32, scores.shape, 1)
        scores = jnp.where(position < lengths[r], scores, -jnp.inf)
        row_max = jnp.maximum(jnp.max(scores, axis=1, keepdims=True), own)
        terms = jnp.exp(scores - row_max)
        own_term = jnp.exp(own - row_max)
        total = jnp.sum(terms, axis=1, keepdims=True) + own_term
        weights = (terms / total).astype(jnp.bfloat16)
        weighted.append((weights, (own_term / total).astype(jnp.bfloat16).astype(jnp.float32)))
    for r in range(rows_here):
        weights, own_weight = weighted[r]
        outs = []
        for j in range(KEY_VALUE_HEADS):
            cols = slice(j * HEAD_SIZE, (j + 1) * HEAD_SIZE)
            outs.append(
                jnp.dot(
                    weights[j * group : (j + 1) * group],
                    v_buf[r, :, cols],
                    preferred_element_type=jnp.float32,
                )
            )
        result = jnp.concatenate(outs, axis=0) + own_weight * staged[r][2]
        mixed[r] = result.astype(jnp.bfloat16).reshape(mixed.shape[1:])

    pl.semaphore_wait(barrier, len(peers))
    moves = []
    for n, (i, j) in enumerate(peers):
        moves.append(
            send(
                mixed.at[:, blk_peer(i)],
                heads_all.at[b, s],
                heads_send.at[n],
                heads_recv.at[n],
                {"blk": blk_peer(i), "sum": sum_peer(j)},
            )
        )
    for copy in moves:
        copy.start()
    heads_all[b, s] = mixed[:, b]

    def turn(t, carry):
        load_gate(t).wait()
        span = pl.ds(pl.multiple_of(t * TILE, TILE), TILE)
        for g in range(2):
            for f in range(columns // TILE):
                cols = slice(f * TILE, (f + 1) * TILE)
                wg[g, span, cols] = wg[g, span, cols].T
        return carry

    lax.fori_loop(0, turns[0], turn, 0)
    for n, (i, j) in enumerate(peers):
        moves[n].wait_send()
        other_b, other_s = lax.rem(b + n_blk - i, n_blk), lax.rem(s + n_sum - j, n_sum)
        send(
            mixed.at[:, blk_peer(i)],
            heads_all.at[other_b, other_s],
            heads_send.at[n],
            heads_recv.at[n],
            {"blk": blk_peer(i), "sum": sum_peer(j)},
        ).wait_recv()
    heads_f32[...] = heads_all[...].astype(jnp.float32).reshape(heads_f32.shape)
    per_block = wo.shape[0] // HEAD_SIZE
    rows_all = n_blk * n_sum * rows_here
    picked = jnp.concatenate(
        [
            heads_f32[pl.ds(h, rows_all, stride=per_block), :].astype(jnp.bfloat16)
            for h in range(per_block)
        ],
        axis=1,
    )
    for copy in load_out:
        copy.wait()
    parts = column_parts(columns)
    moves = []
    for p, (first_col, width) in enumerate(parts):
        cols = pl.ds(first_col, width)
        projected = jnp.dot(picked, wo[:, cols], preferred_element_type=jnp.float32)
        proj_out[:, :, cols] = projected.reshape(n_blk, -1, width).astype(jnp.bfloat16)
        moves.append(
            [
                send(
                    proj_out.at[blk_peer(k), :, cols],
                    proj_in.at[k - 1, :, cols],
                    proj_send.at[p * (n_blk - 1) + k - 1],
                    proj_recv.at[p * (n_blk - 1) + k - 1],
                    {"blk": blk_peer(k)},
                )
                for k in range(1, n_blk)
            ]
        )
        for copy in moves[p]:
            copy.start()
    lax.fori_loop(turns[0], turns[1], turn, 0)
    first[4].wait()
    first[5].wait()
    norm_moves = []
    square_sum = 0.0
    for p, (first_col, width) in enumerate(parts):
        cols = pl.ds(first_col, width)
        total = hidden_buf[:, cols] + proj_out[b, :, cols].astype(jnp.float32)
        for k in range(1, n_blk):
            moves[p][k - 1].wait()
            total = total + proj_in[k - 1, :, cols].astype(jnp.float32)
        residual[:, cols] = total
        scaled = [
            total[:, n : n + 128] * gain_buf[(first_col + n) // 128 : (first_col + n) // 128 + 1, :]
            for n in range(0, width, 128)
        ]
        normed[b, :, cols] = jnp.concatenate(scaled, axis=1).astype(jnp.bfloat16)
        norm_moves.append(
            [
                send(
                    normed.at[b, :, cols],
                    normed.at[b, :, cols],
                    norm_send.at[p * (n_blk - 1) + k - 1],
                    norm_recv.at[p * (n_blk - 1) + k - 1],
                    {"blk": blk_peer(k)},
                )
                for k in range(1, n_blk)
            ]
        )
        for copy in norm_moves[p]:
            copy.start()
        square_sum = square_sum + jnp.sum(total * total, axis=1, keepdims=True)
    squares[s] = jnp.broadcast_to(square_sum, squares.shape[1:])
    square_moves = [
        send(
            squares.at[s],
            squares.at[s],
            square_send.at[k - 1],
            square_recv.at[k - 1],
            {"sum": sum_peer(k)},
        )
        for k in range(1, n_sum)
    ]
    for copy in square_moves:
        copy.start()

    def settle(copies, buffer, send_sems, recv_sems):
        for k in range(1, n_blk):
            copies[k - 1].wait_send()
            other = lax.rem(b + n_blk - k, n_blk)
            send(
                buffer.at[other],
                buffer.at[other],
                send_sems.at[k - 1],
                recv_sems.at[k - 1],
                {"blk": blk_peer(k)},
            ).wait_recv()

    lax.fori_loop(turns[1], tiles, turn, 0)
    for k in range(1, n_sum):
        square_moves[k - 1].wait_send()
        other = lax.rem(s + n_sum - k, n_sum)
        send(
            squares.at[other],
            squares.at[other],
            square_send.at[k - 1],
            square_recv.at[k - 1],
            {"sum": sum_peer(k)},
        ).wait_recv()
    inverse[b] = lax.rsqrt(jnp.sum(squares[...], axis=0) / D + 1e-06)
    inverse_moves = [
        send(
            inverse.at[b],
            inverse.at[b],
            inverse_send.at[k - 1],
            inverse_recv.at[k - 1],
            {"blk": blk_peer(k)},
        )
        for k in range(1, n_blk)
    ]
    for copy in inverse_moves:
        copy.start()
    for p, (first_col, width) in enumerate(parts):
        for k in range(1, n_blk):
            norm_moves[p][k - 1].wait_send()
            there = normed.at[lax.rem(b + n_blk - k, n_blk), :, pl.ds(first_col, width)]
            n = p * (n_blk - 1) + k - 1
            send(there, there, norm_send.at[n], norm_recv.at[n], {"blk": blk_peer(k)}).wait_recv()
    features = normed[...].astype(jnp.float32).reshape(rows_all, columns).astype(jnp.bfloat16)
    half = rows_all // 2
    to_core = [
        send(
            pre_part.at[1 - core, spans[c]],
            pre_core.at[spans[c]],
            core_send.at[c],
            core_recv.at[c],
            {"sum": core_peer},
        )
        for c in range(chunks)
    ]
    to_far = [
        send(
            pre_send.at[spans[c]],
            pre_far.at[spans[c]],
            far_send.at[c],
            far_recv.at[c],
            {"sum": far_peer},
        )
        for c in range(chunks)
    ]
    spread = [
        send(
            act.at[core, spans[c]],
            act.at[core, spans[c]],
            act_send.at[c],
            act_recv.at[c],
            {"sum": core_peer},
        )
        for c in range(chunks)
    ]

    def gate_tile(t):
        u = t * TILE
        for g in range(2):
            turned = jnp.concatenate(
                [wg[g, u : u + TILE, f : f + TILE] for f in range(0, columns, TILE)], axis=0
            )
            value = jnp.dot(features, turned, preferred_element_type=jnp.float32)
            value = value.astype(jnp.bfloat16)
            pre_part[0, t, g] = value[:half]
            pre_part[1, t, g] = value[half:]

    def core_part(c):
        to_core[c].wait()
        added = pre_part[core, spans[c]].astype(jnp.float32) + pre_core[spans[c]].astype(
            jnp.float32
        )
        pre_sum[spans[c]] = added
        pre_send[spans[c]] = added.astype(jnp.bfloat16)
        to_far[c].start()

    def act_part(c):
        to_far[c].wait()
        total = pre_sum[spans[c]] + pre_far[spans[c]].astype(jnp.float32)
        gate = total[:, 0] * factor
        up = total[:, 1] * factor
        act[core, spans[c]] = (gate / (1.0 + jnp.exp(-gate)) * up).astype(jnp.bfloat16)
        spread[c].start()

    def down_part(c):
        spread[c].wait_send()
        send(
            act.at[1 - core, spans[c]],
            act.at[1 - core, spans[c]],
            act_send.at[c],
            act_recv.at[c],
            {"sum": core_peer},
        ).wait_recv()
        span = range(ends[c] - sizes[c], ends[c])
        for t in span:
            load_down(t).wait()
        value = jnp.dot(
            jnp.concatenate([act[:, t].reshape(rows_all, TILE) for t in span], axis=1),
            wd[pl.ds(span[0] * TILE, sizes[c] * TILE), :],
            preferred_element_type=jnp.float32,
        )
        if c > 0:
            value = value + down_acc[...]
        down_acc[...] = value

    ready = 0
    for t in range(tiles):
        gate_tile(t)
        if t + 1 in ends:
            done = ends.index(t + 1)
            to_core[done].start()
            if done >= 1:
                core_part(done - 1)
                ready = done
    for c in range(ready, chunks):
        core_part(c)
    settle(inverse_moves, inverse, inverse_send, inverse_recv)
    factor = inverse[pl.ds((n_blk // 2) * core, n_blk // 2)].reshape(half, 128)[:, :1]
    for step in range(chunks + DOWN_LAG):
        if step < chunks:
            act_part(step)
        if step >= DOWN_LAG:
            down_part(step - DOWN_LAG)
    down_out[...] = down_acc[...].reshape(down_out.shape).astype(jnp.bfloat16)
    moves = [
        send(
            down_out.at[blk_peer(k)],
            down_in.at[k - 1],
            down_send.at[k - 1],
            down_recv.at[k - 1],
            {"blk": blk_peer(k)},
        )
        for k in range(1, n_blk)
    ]
    for copy in moves:
        copy.start()
    total = residual[...] + down_out[b].astype(jnp.float32)
    for k in range(1, n_blk):
        moves[k - 1].wait()
        total = total + down_in[k - 1].astype(jnp.float32)
    out_ref[...] = total


def column_parts(columns):
    first = TILE * -(-columns // (2 * TILE))
    return [(0, first), (first, columns - first)]


def turn_counts(tiles):
    return [2 * tiles // 5, 16 * tiles // 25]


def chunk_sizes(units):
    tiles = units // TILE
    first, last = [2, 4], [4]
    middle = tiles - sum(first + last)
    parts = -(-middle // 5)
    sizes = [middle // parts + (i < middle % parts) for i in range(parts)]
    return first + sizes + last


def kernel_fits(queries, hidden, out_weight, gate_up_weight):
    n_blk, n_sum = lax.axis_size("blk"), lax.axis_size("sum")
    units, columns = gate_up_weight.shape[1:]
    weights = 2 * (out_weight.size + gate_up_weight.size + units * columns)
    return (
        n_sum == 4
        and n_blk % 2 == 0
        and queries.shape[0] == 2
        and hidden.shape[0] == 8
        and out_weight.shape[0] % (16 * HEAD_SIZE) == 0
        and units % 256 == 0
        and units >= 13 * 256
        and columns % 256 == 0
        and columns >= 512
        and weights <= 53 * 2**20
    )


def layer_in_kernel(
    queries,
    cached_key_rows,
    cached_value_rows,
    incoming_pairs,
    cache_length,
    hidden,
    norm_gain,
    out_weight,
    gate_up_weight,
    down_weight,
):
    n_blk, n_sum = lax.axis_size("blk"), lax.axis_size("sum")
    rows = queries.shape[0]
    own_rows, columns = hidden.shape
    rows_all = n_blk * own_rows
    units = down_weight.shape[0]
    chunks = len(chunk_sizes(units))
    per_block = out_weight.shape[0] // HEAD_SIZE
    bf16, f32 = jnp.bfloat16, jnp.float32
    anywhere = pl.BlockSpec(memory_space=pl.ANY)
    tiles = units // TILE
    sems = [6, WO_PIECES, tiles, tiles]
    sems += [n_blk * n_sum - 1] * 2 + [2 * (n_blk - 1)] * 4 + [n_sum - 1] * 2
    sems += [n_blk - 1] * 2 + [chunks] * 6 + [n_blk - 1] * 2
    gain = norm_gain.reshape(columns // 128, 128)
    like = lambda x: pltpu.VMEM(x.shape, x.dtype)
    half = rows_all // 2
    return pl.pallas_call(
        layer_kernel,
        out_shape=pltpu.VMEM(hidden.shape, f32),
        in_specs=[pl.BlockSpec(memory_space=pltpu.SMEM)] + [anywhere] * 9,
        out_specs=pl.BlockSpec(memory_space=pltpu.VMEM),
        scratch_shapes=[
            like(queries),
            like(cached_key_rows),
            like(cached_value_rows),
            like(incoming_pairs),
            like(hidden),
            like(gain),
            like(out_weight),
            like(gate_up_weight),
            like(down_weight),
            pltpu.VMEM((rows, QUERY_HEADS, HEAD_SIZE), f32),
            pltpu.VMEM((rows, n_blk, per_block, HEAD_SIZE), bf16),
            pltpu.VMEM((n_blk, n_sum, rows, per_block, HEAD_SIZE), bf16),
            pltpu.VMEM((rows_all * per_block, HEAD_SIZE), f32),
            pltpu.VMEM((n_blk, own_rows, columns), bf16),
            pltpu.VMEM((n_blk - 1, own_rows, columns), bf16),
            pltpu.VMEM(hidden.shape, f32),
            pltpu.VMEM((n_blk, own_rows, columns), bf16),
            pltpu.VMEM((n_sum, own_rows, 128), f32),
            pltpu.VMEM((n_blk, own_rows, 128), f32),
            pltpu.VMEM((2, tiles, 2, half, TILE), bf16),
            pltpu.VMEM((tiles, 2, half, TILE), bf16),
            pltpu.VMEM((tiles, 2, half, TILE), f32),
            pltpu.VMEM((tiles, 2, half, TILE), bf16),
            pltpu.VMEM((tiles, 2, half, TILE), bf16),
            pltpu.VMEM((2, tiles, half, TILE), bf16),
            pltpu.VMEM((rows_all, columns), f32),
            pltpu.VMEM((n_blk, own_rows, columns), bf16),
            pltpu.VMEM((n_blk - 1, own_rows, columns), bf16),
        ]
        + [pltpu.SemaphoreType.DMA((n,)) for n in sems],
        compiler_params=pltpu.CompilerParams(
            collective_id=0, has_side_effects=True, vmem_limit_bytes=60 * 2**20
        ),
    )(
        cache_length,
        queries,
        cached_key_rows,
        cached_value_rows,
        incoming_pairs,
        hidden,
        gain,
        out_weight,
        gate_up_weight,
        down_weight,
    )


def on_device(
    queries,
    cached_key_rows,
    cached_value_rows,
    incoming_pairs,
    cache_length,
    hidden,
    norm_gain,
    out_weight,
    gate_up_weight,
    down_weight,
):
    if kernel_fits(queries, hidden, out_weight, gate_up_weight):
        return layer_in_kernel(
            queries,
            cached_key_rows,
            cached_value_rows,
            incoming_pairs,
            cache_length,
            hidden,
            norm_gain,
            out_weight,
            gate_up_weight,
            down_weight,
        )
    attended = attend_padded(
        queries, cached_key_rows, cached_value_rows, incoming_pairs, cache_length
    )
    spread = lax.all_to_all(attended, "blk", split_axis=1, concat_axis=0, tiled=True)
    spread = spread.reshape(lax.axis_size("blk"), attended.shape[0], spread.shape[1])
    heads_rows = lax.all_gather(spread, "sum", axis=1, tiled=True).reshape(-1, spread.shape[2])
    picked = heads_rows
    projected = lax.psum_scatter(
        jnp.dot(picked, out_weight, preferred_element_type=jnp.float32).astype(jnp.bfloat16),
        "blk",
        scatter_dimension=0,
        tiled=True,
    ).astype(jnp.float32)
    residual = hidden + projected
    square_sum = lax.psum(jnp.sum(residual * residual, axis=1), "sum")
    inverse = lax.rsqrt(square_sum / D + 1e-06)
    normed = (residual * inverse[:, None] * norm_gain[None, :]).astype(jnp.bfloat16)
    pre_terms = jnp.einsum(
        "nd,gfd->ngf",
        lax.all_gather(normed, "blk", axis=0, tiled=True),
        gate_up_weight,
        preferred_element_type=jnp.float32,
    )
    summed = lax.psum(pre_terms.astype(jnp.bfloat16), "sum").astype(jnp.float32)
    activated = (jax.nn.silu(summed[:, 0]) * summed[:, 1]).astype(jnp.bfloat16)
    picked = activated
    feed_sum = lax.psum_scatter(
        jnp.dot(picked, down_weight, preferred_element_type=jnp.float32).astype(jnp.bfloat16),
        "blk",
        scatter_dimension=0,
        tiled=True,
    ).astype(jnp.float32)
    return residual + feed_sum


def solution(mesh):
    placed = (
        P(("groups", "blk", "sum"), None),
        P(("groups", "blk", "sum"), None, None),
        P(("groups", "blk", "sum"), None, None),
        P(("groups", "blk", "sum"), None, None),
        P(("groups", "blk", "sum")),
        P(("groups", "blk"), "sum"),
        P("sum"),
        P("blk", "sum"),
        P(None, "blk", "sum"),
        P("blk", "sum"),
    )
    return jax.shard_map(
        on_device,
        mesh=mesh,
        in_specs=placed,
        out_specs=P(("groups", "blk"), "sum"),
        check_vma=False,
    )
```

```python
import jax
import jax.numpy as jnp
from jax import lax
from jax.experimental import pallas as pl
from jax.experimental.pallas import tpu as pltpu
from jax.sharding import PartitionSpec as P

D = 5120
QUERY_HEADS = 64
KEY_VALUE_HEADS = 8
HEAD_SIZE = 128
CACHE_SLOTS = 128


def attend_padded(queries, cached_key_rows, cached_value_rows, incoming_pairs, cache_length):
    count_of_rows = queries.shape[0]
    score_scale = HEAD_SIZE ** (-0.5)
    query_head_count = queries.reshape(
        count_of_rows, KEY_VALUE_HEADS, QUERY_HEADS // KEY_VALUE_HEADS, HEAD_SIZE
    )
    key_head_count = cached_key_rows.reshape(count_of_rows, CACHE_SLOTS, KEY_VALUE_HEADS, HEAD_SIZE)
    value_head_count = cached_value_rows.reshape(
        count_of_rows, CACHE_SLOTS, KEY_VALUE_HEADS, HEAD_SIZE
    )
    incoming_key = incoming_pairs[:, 0].reshape(count_of_rows, KEY_VALUE_HEADS, HEAD_SIZE)
    incoming_value = incoming_pairs[:, 1].reshape(count_of_rows, KEY_VALUE_HEADS, HEAD_SIZE)
    scores = (
        jnp.einsum(
            "nkgd,nlkd->nkgl", query_head_count, key_head_count, preferred_element_type=jnp.float32
        )
        * score_scale
    )
    own_score = (
        jnp.einsum(
            "nkgd,nkd->nkg", query_head_count, incoming_key, preferred_element_type=jnp.float32
        )
        * score_scale
    )
    live_mask = jnp.arange(CACHE_SLOTS)[None, :] < cache_length[:, None]
    scores = jnp.where(live_mask[:, None, None, :], scores, -jnp.inf)
    row_max = jnp.maximum(jnp.max(scores, axis=-1), own_score)
    cache_terms = jnp.exp(scores - row_max[..., None])
    own_term = jnp.exp(own_score - row_max)
    row_total = jnp.sum(cache_terms, axis=-1) + own_term
    weights = (cache_terms / row_total[..., None]).astype(jnp.bfloat16)
    own_weight = (own_term / row_total).astype(jnp.bfloat16)
    mixed = jnp.einsum(
        "nkgl,nlkd->nkgd", weights, value_head_count, preferred_element_type=jnp.float32
    )
    mixed = (
        mixed
        + own_weight.astype(jnp.float32)[..., None]
        * incoming_value.astype(jnp.float32)[:, :, None, :]
    )
    return mixed.astype(jnp.bfloat16).reshape(count_of_rows, QUERY_HEADS * HEAD_SIZE)


MESH = pl.DeviceIdType.MESH


TILE = 256
WO_PIECES = 8
DOWN_LAG = 1


def layer_kernel(
    lengths,
    q_hbm,
    k_hbm,
    v_hbm,
    pair_hbm,
    hidden_hbm,
    gain_hbm,
    wo_hbm,
    wg_hbm,
    wd_hbm,
    out_ref,
    q_buf,
    k_buf,
    v_buf,
    pair_buf,
    hidden_buf,
    gain_buf,
    wo,
    wg,
    wd,
    q_rows,
    mixed,
    heads_all,
    heads_f32,
    proj_out,
    proj_in,
    residual,
    normed,
    squares,
    inverse,
    pre_part,
    pre_core,
    pre_sum,
    pre_send,
    pre_far,
    act,
    down_acc,
    down_out,
    down_in,
    load_sem,
    wo_sem,
    wg_sem,
    wd_sem,
    heads_send,
    heads_recv,
    proj_send,
    proj_recv,
    norm_send,
    norm_recv,
    square_send,
    square_recv,
    inverse_send,
    inverse_recv,
    core_send,
    core_recv,
    far_send,
    far_recv,
    act_send,
    act_recv,
    down_send,
    down_recv,
):
    n_blk, n_sum = lax.axis_size("blk"), lax.axis_size("sum")
    rows_here = q_buf.shape[0]
    units, columns = wd.shape
    tiles = units // TILE
    sizes = chunk_sizes(units)
    chunks = len(sizes)
    ends = [sum(sizes[: c + 1]) for c in range(chunks)]
    spans = [pl.ds(ends[c] - sizes[c], sizes[c]) for c in range(chunks)]
    b, s = lax.axis_index("blk"), lax.axis_index("sum")
    core = lax.rem(s, 2)
    core_peer = s + 1 - 2 * core
    far_peer = lax.rem(s + 2, n_sum)

    def blk_peer(k):
        return lax.rem(b + k, n_blk)

    def sum_peer(k):
        return lax.rem(s + k, n_sum)

    def send(src, dst, send_sem, recv_sem, where):
        return pltpu.make_async_remote_copy(
            src_ref=src,
            dst_ref=dst,
            send_sem=send_sem,
            recv_sem=recv_sem,
            device_id=where,
            device_id_type=MESH,
        )

    blk_order = [n_blk // 2] + [k for k in range(1, n_blk) if k != n_blk // 2]
    peers = [(i, j) for i in blk_order + [0] for j in (2, 3, 1, 0) if (i, j) != (0, 0)]

    barrier = pltpu.get_barrier_semaphore()
    first = [
        pltpu.make_async_copy(src, dst, load_sem.at[i])
        for i, (src, dst) in enumerate(
            [
                (q_hbm, q_buf),
                (k_hbm, k_buf),
                (pair_hbm, pair_buf),
                (v_hbm, v_buf),
                (hidden_hbm, hidden_buf),
                (gain_hbm, gain_buf),
            ]
        )
    ]

    def load_gate(t):
        span = pl.ds(pl.multiple_of(t * TILE, TILE), TILE)
        return pltpu.make_async_copy(wg_hbm.at[:, span, :], wg.at[:, span, :], wg_sem.at[t])

    def load_down(t):
        span = pl.ds(pl.multiple_of(t * TILE, TILE), TILE)
        return pltpu.make_async_copy(wd_hbm.at[span, :], wd.at[span, :], wd_sem.at[t])

    piece = wo.shape[0] // WO_PIECES
    load_out = [
        pltpu.make_async_copy(
            wo_hbm.at[pl.ds(i * piece, piece), :], wo.at[pl.ds(i * piece, piece), :], wo_sem.at[i]
        )
        for i in range(WO_PIECES)
    ]
    for copy in first[:4]:
        copy.start()
    for i, j in peers:
        pl.semaphore_signal(
            barrier,
            inc=1,
            device_id={"blk": blk_peer(i), "sum": sum_peer(j)},
            device_id_type=MESH,
        )
    first[0].wait()
    for copy in load_out + first[4:]:
        copy.start()
    for copy in first[1:4]:
        copy.wait()
    turns = turn_counts(tiles)

    def start_gate(t, carry):
        load_gate(t).start()
        return carry

    def start_down(t, carry):
        load_down(t).start()
        return carry

    lax.fori_loop(0, tiles, start_gate, 0)
    lax.fori_loop(0, tiles, start_down, 0)

    group = QUERY_HEADS // KEY_VALUE_HEADS
    queries = q_buf[...].astype(jnp.float32)
    for r in range(rows_here):
        for h in range(QUERY_HEADS):
            q_rows[r, h : h + 1, :] = queries[r : r + 1, h * HEAD_SIZE : (h + 1) * HEAD_SIZE]
    score_scale = HEAD_SIZE ** (-0.5)
    staged = []
    for r in range(rows_here):
        q32 = q_rows[r]
        q16 = q32.astype(jnp.bfloat16)
        new_key = pair_buf[r, 0:1, :].astype(jnp.float32)
        new_value = pair_buf[r, 1:2, :].astype(jnp.float32)
        scores, keys_new, values_new = [], [], []
        for j in range(KEY_VALUE_HEADS):
            cols = slice(j * HEAD_SIZE, (j + 1) * HEAD_SIZE)
            scores.append(
                lax.dot_general(
                    q16[j * group : (j + 1) * group],
                    k_buf[r, :, cols],
                    (((1,), (1,)), ((), ())),
                    preferred_element_type=jnp.float32,
                )
            )
            keys_new.append(jnp.broadcast_to(new_key[:, cols], (group, HEAD_SIZE)))
            values_new.append(jnp.broadcast_to(new_value[:, cols], (group, HEAD_SIZE)))
        scores = jnp.concatenate(scores, axis=0) * score_scale
        own = jnp.sum(q32 * jnp.concatenate(keys_new, axis=0), axis=1, keepdims=True) * score_scale
        staged.append((scores, own, jnp.concatenate(values_new, axis=0)))
    weighted = []
    for r in range(rows_here):
        scores, own, _ = staged[r]
        position = lax.broadcasted_iota(jnp.int32, scores.shape, 1)
        scores = jnp.where(position < lengths[r], scores, -jnp.inf)
        row_max = jnp.maximum(jnp.max(scores, axis=1, keepdims=True), own)
        terms = jnp.exp(scores - row_max)
        own_term = jnp.exp(own - row_max)
        total = jnp.sum(terms, axis=1, keepdims=True) + own_term
        weights = (terms / total).astype(jnp.bfloat16)
        weighted.append((weights, (own_term / total).astype(jnp.bfloat16).astype(jnp.float32)))
    for r in range(rows_here):
        weights, own_weight = weighted[r]
        outs = []
        for j in range(KEY_VALUE_HEADS):
            cols = slice(j * HEAD_SIZE, (j + 1) * HEAD_SIZE)
            outs.append(
                jnp.dot(
                    weights[j * group : (j + 1) * group],
                    v_buf[r, :, cols],
                    preferred_element_type=jnp.float32,
                )
            )
        result = jnp.concatenate(outs, axis=0) + own_weight * staged[r][2]
        mixed[r] = result.astype(jnp.bfloat16).reshape(mixed.shape[1:])

    pl.semaphore_wait(barrier, len(peers))
    moves = []
    for n, (i, j) in enumerate(peers):
        moves.append(
            send(
                mixed.at[:, blk_peer(i)],
                heads_all.at[b, s],
                heads_send.at[n],
                heads_recv.at[n],
                {"blk": blk_peer(i), "sum": sum_peer(j)},
            )
        )
    for copy in moves:
        copy.start()
    heads_all[b, s] = mixed[:, b]

    def turn(t, carry):
        load_gate(t).wait()
        span = pl.ds(pl.multiple_of(t * TILE, TILE), TILE)
        for g in range(2):
            for f in range(columns // TILE):
                cols = slice(f * TILE, (f + 1) * TILE)
                wg[g, span, cols] = wg[g, span, cols].T
        return carry

    lax.fori_loop(0, turns[0], turn, 0)
    for n, (i, j) in enumerate(peers):
        moves[n].wait_send()
        other_b, other_s = lax.rem(b + n_blk - i, n_blk), lax.rem(s + n_sum - j, n_sum)
        send(
            mixed.at[:, blk_peer(i)],
            heads_all.at[other_b, other_s],
            heads_send.at[n],
            heads_recv.at[n],
            {"blk": blk_peer(i), "sum": sum_peer(j)},
        ).wait_recv()
    heads_f32[...] = heads_all[...].astype(jnp.float32).reshape(heads_f32.shape)
    per_block = wo.shape[0] // HEAD_SIZE
    rows_all = n_blk * n_sum * rows_here
    picked = jnp.concatenate(
        [
            heads_f32[pl.ds(h, rows_all, stride=per_block), :].astype(jnp.bfloat16)
            for h in range(per_block)
        ],
        axis=1,
    )
    for copy in load_out:
        copy.wait()
    parts = column_parts(columns)
    moves = []
    for p, (first_col, width) in enumerate(parts):
        cols = pl.ds(first_col, width)
        projected = jnp.dot(picked, wo[:, cols], preferred_element_type=jnp.float32)
        proj_out[:, :, cols] = projected.reshape(n_blk, -1, width).astype(jnp.bfloat16)
        moves.append(
            [
                send(
                    proj_out.at[blk_peer(k), :, cols],
                    proj_in.at[k - 1, :, cols],
                    proj_send.at[p * (n_blk - 1) + k - 1],
                    proj_recv.at[p * (n_blk - 1) + k - 1],
                    {"blk": blk_peer(k)},
                )
                for k in range(1, n_blk)
            ]
        )
        for copy in moves[p]:
            copy.start()
    lax.fori_loop(turns[0], turns[1], turn, 0)
    first[4].wait()
    first[5].wait()
    norm_moves = []
    square_sum = 0.0
    for p, (first_col, width) in enumerate(parts):
        cols = pl.ds(first_col, width)
        total = hidden_buf[:, cols] + proj_out[b, :, cols].astype(jnp.float32)
        for k in range(1, n_blk):
            moves[p][k - 1].wait()
            total = total + proj_in[k - 1, :, cols].astype(jnp.float32)
        residual[:, cols] = total
        scaled = [
            total[:, n : n + 128] * gain_buf[(first_col + n) // 128 : (first_col + n) // 128 + 1, :]
            for n in range(0, width, 128)
        ]
        normed[b, :, cols] = jnp.concatenate(scaled, axis=1).astype(jnp.bfloat16)
        norm_moves.append(
            [
                send(
                    normed.at[b, :, cols],
                    normed.at[b, :, cols],
                    norm_send.at[p * (n_blk - 1) + k - 1],
                    norm_recv.at[p * (n_blk - 1) + k - 1],
                    {"blk": blk_peer(k)},
                )
                for k in range(1, n_blk)
            ]
        )
        for copy in norm_moves[p]:
            copy.start()
        square_sum = square_sum + jnp.sum(total * total, axis=1, keepdims=True)
    squares[s] = jnp.broadcast_to(square_sum, squares.shape[1:])
    square_moves = [
        send(
            squares.at[s],
            squares.at[s],
            square_send.at[k - 1],
            square_recv.at[k - 1],
            {"sum": sum_peer(k)},
        )
        for k in range(1, n_sum)
    ]
    for copy in square_moves:
        copy.start()

    def settle(copies, buffer, send_sems, recv_sems):
        for k in range(1, n_blk):
            copies[k - 1].wait_send()
            other = lax.rem(b + n_blk - k, n_blk)
            send(
                buffer.at[other],
                buffer.at[other],
                send_sems.at[k - 1],
                recv_sems.at[k - 1],
                {"blk": blk_peer(k)},
            ).wait_recv()

    lax.fori_loop(turns[1], tiles, turn, 0)
    for k in range(1, n_sum):
        square_moves[k - 1].wait_send()
        other = lax.rem(s + n_sum - k, n_sum)
        send(
            squares.at[other],
            squares.at[other],
            square_send.at[k - 1],
            square_recv.at[k - 1],
            {"sum": sum_peer(k)},
        ).wait_recv()
    inverse[b] = lax.rsqrt(jnp.sum(squares[...], axis=0) / D + 1e-06)
    inverse_moves = [
        send(
            inverse.at[b],
            inverse.at[b],
            inverse_send.at[k - 1],
            inverse_recv.at[k - 1],
            {"blk": blk_peer(k)},
        )
        for k in range(1, n_blk)
    ]
    for copy in inverse_moves:
        copy.start()
    for p, (first_col, width) in enumerate(parts):
        for k in range(1, n_blk):
            norm_moves[p][k - 1].wait_send()
            there = normed.at[lax.rem(b + n_blk - k, n_blk), :, pl.ds(first_col, width)]
            n = p * (n_blk - 1) + k - 1
            send(there, there, norm_send.at[n], norm_recv.at[n], {"blk": blk_peer(k)}).wait_recv()
    features = normed[...].astype(jnp.float32).reshape(rows_all, columns).astype(jnp.bfloat16)
    half = rows_all // 2
    to_core = [
        send(
            pre_part.at[1 - core, spans[c]],
            pre_core.at[spans[c]],
            core_send.at[c],
            core_recv.at[c],
            {"sum": core_peer},
        )
        for c in range(chunks)
    ]
    to_far = [
        send(
            pre_send.at[spans[c]],
            pre_far.at[spans[c]],
            far_send.at[c],
            far_recv.at[c],
            {"sum": far_peer},
        )
        for c in range(chunks)
    ]
    spread = [
        send(
            act.at[core, spans[c]],
            act.at[core, spans[c]],
            act_send.at[c],
            act_recv.at[c],
            {"sum": core_peer},
        )
        for c in range(chunks)
    ]

    def gate_tile(t):
        u = t * TILE
        for g in range(2):
            turned = jnp.concatenate(
                [wg[g, u : u + TILE, f : f + TILE] for f in range(0, columns, TILE)], axis=0
            )
            value = jnp.dot(features, turned, preferred_element_type=jnp.float32)
            value = value.astype(jnp.bfloat16)
            pre_part[0, t, g] = value[:half]
            pre_part[1, t, g] = value[half:]

    def core_part(c):
        to_core[c].wait()
        added = pre_part[core, spans[c]].astype(jnp.float32) + pre_core[spans[c]].astype(
            jnp.float32
        )
        pre_sum[spans[c]] = added
        pre_send[spans[c]] = added.astype(jnp.bfloat16)
        to_far[c].start()

    def act_part(c):
        to_far[c].wait()
        total = pre_sum[spans[c]] + pre_far[spans[c]].astype(jnp.float32)
        gate = total[:, 0] * factor
        up = total[:, 1] * factor
        act[core, spans[c]] = (gate / (1.0 + jnp.exp(-gate)) * up).astype(jnp.bfloat16)
        spread[c].start()

    def down_part(c):
        spread[c].wait_send()
        send(
            act.at[1 - core, spans[c]],
            act.at[1 - core, spans[c]],
            act_send.at[c],
            act_recv.at[c],
            {"sum": core_peer},
        ).wait_recv()
        span = range(ends[c] - sizes[c], ends[c])
        for t in span:
            load_down(t).wait()
        value = jnp.dot(
            jnp.concatenate([act[:, t].reshape(rows_all, TILE) for t in span], axis=1),
            wd[pl.ds(span[0] * TILE, sizes[c] * TILE), :],
            preferred_element_type=jnp.float32,
        )
        if c > 0:
            value = value + down_acc[...]
        down_acc[...] = value

    ready = 0
    for t in range(tiles):
        gate_tile(t)
        if t + 1 in ends:
            done = ends.index(t + 1)
            to_core[done].start()
            if done >= 1:
                core_part(done - 1)
                ready = done
    for c in range(ready, chunks):
        core_part(c)
    settle(inverse_moves, inverse, inverse_send, inverse_recv)
    factor = inverse[pl.ds((n_blk // 2) * core, n_blk // 2)].reshape(half, 128)[:, :1]
    for step in range(chunks + DOWN_LAG):
        if step < chunks:
            act_part(step)
        if step >= DOWN_LAG:
            down_part(step - DOWN_LAG)
    down_out[...] = down_acc[...].reshape(down_out.shape).astype(jnp.bfloat16)
    moves = [
        send(
            down_out.at[blk_peer(k)],
            down_in.at[k - 1],
            down_send.at[k - 1],
            down_recv.at[k - 1],
            {"blk": blk_peer(k)},
        )
        for k in range(1, n_blk)
    ]
    for copy in moves:
        copy.start()
    total = residual[...] + down_out[b].astype(jnp.float32)
    for k in range(1, n_blk):
        moves[k - 1].wait()
        total = total + down_in[k - 1].astype(jnp.float32)
    out_ref[...] = total


def column_parts(columns):
    first = TILE * -(-columns // (2 * TILE))
    return [(0, first), (first, columns - first)]


def turn_counts(tiles):
    return [2 * tiles // 5, 16 * tiles // 25]


def chunk_sizes(units):
    tiles = units // TILE
    first, last = [3], [3]
    middle = tiles - sum(first + last)
    parts = -(-middle // 5)
    sizes = [middle // parts + (i < middle % parts) for i in range(parts)]
    return first + sizes + last


def kernel_fits(queries, hidden, out_weight, gate_up_weight):
    n_blk, n_sum = lax.axis_size("blk"), lax.axis_size("sum")
    units, columns = gate_up_weight.shape[1:]
    weights = 2 * (out_weight.size + gate_up_weight.size + units * columns)
    return (
        n_sum == 4
        and n_blk % 2 == 0
        and queries.shape[0] == 2
        and hidden.shape[0] == 8
        and out_weight.shape[0] % (16 * HEAD_SIZE) == 0
        and units % 256 == 0
        and units >= 13 * 256
        and columns % 256 == 0
        and columns >= 512
        and weights <= 53 * 2**20
    )


def layer_in_kernel(
    queries,
    cached_key_rows,
    cached_value_rows,
    incoming_pairs,
    cache_length,
    hidden,
    norm_gain,
    out_weight,
    gate_up_weight,
    down_weight,
):
    n_blk, n_sum = lax.axis_size("blk"), lax.axis_size("sum")
    rows = queries.shape[0]
    own_rows, columns = hidden.shape
    rows_all = n_blk * own_rows
    units = down_weight.shape[0]
    chunks = len(chunk_sizes(units))
    per_block = out_weight.shape[0] // HEAD_SIZE
    bf16, f32 = jnp.bfloat16, jnp.float32
    anywhere = pl.BlockSpec(memory_space=pl.ANY)
    tiles = units // TILE
    sems = [6, WO_PIECES, tiles, tiles]
    sems += [n_blk * n_sum - 1] * 2 + [2 * (n_blk - 1)] * 4 + [n_sum - 1] * 2
    sems += [n_blk - 1] * 2 + [chunks] * 6 + [n_blk - 1] * 2
    gain = norm_gain.reshape(columns // 128, 128)
    like = lambda x: pltpu.VMEM(x.shape, x.dtype)
    half = rows_all // 2
    return pl.pallas_call(
        layer_kernel,
        out_shape=pltpu.VMEM(hidden.shape, f32),
        in_specs=[pl.BlockSpec(memory_space=pltpu.SMEM)] + [anywhere] * 9,
        out_specs=pl.BlockSpec(memory_space=pltpu.VMEM),
        scratch_shapes=[
            like(queries),
            like(cached_key_rows),
            like(cached_value_rows),
            like(incoming_pairs),
            like(hidden),
            like(gain),
            like(out_weight),
            like(gate_up_weight),
            like(down_weight),
            pltpu.VMEM((rows, QUERY_HEADS, HEAD_SIZE), f32),
            pltpu.VMEM((rows, n_blk, per_block, HEAD_SIZE), bf16),
            pltpu.VMEM((n_blk, n_sum, rows, per_block, HEAD_SIZE), bf16),
            pltpu.VMEM((rows_all * per_block, HEAD_SIZE), f32),
            pltpu.VMEM((n_blk, own_rows, columns), bf16),
            pltpu.VMEM((n_blk - 1, own_rows, columns), bf16),
            pltpu.VMEM(hidden.shape, f32),
            pltpu.VMEM((n_blk, own_rows, columns), bf16),
            pltpu.VMEM((n_sum, own_rows, 128), f32),
            pltpu.VMEM((n_blk, own_rows, 128), f32),
            pltpu.VMEM((2, tiles, 2, half, TILE), bf16),
            pltpu.VMEM((tiles, 2, half, TILE), bf16),
            pltpu.VMEM((tiles, 2, half, TILE), f32),
            pltpu.VMEM((tiles, 2, half, TILE), bf16),
            pltpu.VMEM((tiles, 2, half, TILE), bf16),
            pltpu.VMEM((2, tiles, half, TILE), bf16),
            pltpu.VMEM((rows_all, columns), f32),
            pltpu.VMEM((n_blk, own_rows, columns), bf16),
            pltpu.VMEM((n_blk - 1, own_rows, columns), bf16),
        ]
        + [pltpu.SemaphoreType.DMA((n,)) for n in sems],
        compiler_params=pltpu.CompilerParams(
            collective_id=0, has_side_effects=True, vmem_limit_bytes=60 * 2**20
        ),
    )(
        cache_length,
        queries,
        cached_key_rows,
        cached_value_rows,
        incoming_pairs,
        hidden,
        gain,
        out_weight,
        gate_up_weight,
        down_weight,
    )


def on_device(
    queries,
    cached_key_rows,
    cached_value_rows,
    incoming_pairs,
    cache_length,
    hidden,
    norm_gain,
    out_weight,
    gate_up_weight,
    down_weight,
):
    if kernel_fits(queries, hidden, out_weight, gate_up_weight):
        return layer_in_kernel(
            queries,
            cached_key_rows,
            cached_value_rows,
            incoming_pairs,
            cache_length,
            hidden,
            norm_gain,
            out_weight,
            gate_up_weight,
            down_weight,
        )
    attended = attend_padded(
        queries, cached_key_rows, cached_value_rows, incoming_pairs, cache_length
    )
    spread = lax.all_to_all(attended, "blk", split_axis=1, concat_axis=0, tiled=True)
    spread = spread.reshape(lax.axis_size("blk"), attended.shape[0], spread.shape[1])
    heads_rows = lax.all_gather(spread, "sum", axis=1, tiled=True).reshape(-1, spread.shape[2])
    picked = heads_rows
    projected = lax.psum_scatter(
        jnp.dot(picked, out_weight, preferred_element_type=jnp.float32).astype(jnp.bfloat16),
        "blk",
        scatter_dimension=0,
        tiled=True,
    ).astype(jnp.float32)
    residual = hidden + projected
    square_sum = lax.psum(jnp.sum(residual * residual, axis=1), "sum")
    inverse = lax.rsqrt(square_sum / D + 1e-06)
    normed = (residual * inverse[:, None] * norm_gain[None, :]).astype(jnp.bfloat16)
    pre_terms = jnp.einsum(
        "nd,gfd->ngf",
        lax.all_gather(normed, "blk", axis=0, tiled=True),
        gate_up_weight,
        preferred_element_type=jnp.float32,
    )
    summed = lax.psum(pre_terms.astype(jnp.bfloat16), "sum").astype(jnp.float32)
    activated = (jax.nn.silu(summed[:, 0]) * summed[:, 1]).astype(jnp.bfloat16)
    picked = activated
    feed_sum = lax.psum_scatter(
        jnp.dot(picked, down_weight, preferred_element_type=jnp.float32).astype(jnp.bfloat16),
        "blk",
        scatter_dimension=0,
        tiled=True,
    ).astype(jnp.float32)
    return residual + feed_sum


def solution(mesh):
    placed = (
        P(("groups", "blk", "sum"), None),
        P(("groups", "blk", "sum"), None, None),
        P(("groups", "blk", "sum"), None, None),
        P(("groups", "blk", "sum"), None, None),
        P(("groups", "blk", "sum")),
        P(("groups", "blk"), "sum"),
        P("sum"),
        P("blk", "sum"),
        P(None, "blk", "sum"),
        P("blk", "sum"),
    )
    return jax.shard_map(
        on_device,
        mesh=mesh,
        in_specs=placed,
        out_specs=P(("groups", "blk"), "sum"),
        check_vma=False,
    )
```

```python
import jax
import jax.numpy as jnp
from jax import lax
from jax.experimental import pallas as pl
from jax.experimental.pallas import tpu as pltpu
from jax.sharding import PartitionSpec as P

D = 5120
QUERY_HEADS = 64
KEY_VALUE_HEADS = 8
HEAD_SIZE = 128
CACHE_SLOTS = 128


def attend_padded(queries, cached_key_rows, cached_value_rows, incoming_pairs, cache_length):
    count_of_rows = queries.shape[0]
    score_scale = HEAD_SIZE ** (-0.5)
    query_head_count = queries.reshape(
        count_of_rows, KEY_VALUE_HEADS, QUERY_HEADS // KEY_VALUE_HEADS, HEAD_SIZE
    )
    key_head_count = cached_key_rows.reshape(count_of_rows, CACHE_SLOTS, KEY_VALUE_HEADS, HEAD_SIZE)
    value_head_count = cached_value_rows.reshape(
        count_of_rows, CACHE_SLOTS, KEY_VALUE_HEADS, HEAD_SIZE
    )
    incoming_key = incoming_pairs[:, 0].reshape(count_of_rows, KEY_VALUE_HEADS, HEAD_SIZE)
    incoming_value = incoming_pairs[:, 1].reshape(count_of_rows, KEY_VALUE_HEADS, HEAD_SIZE)
    scores = (
        jnp.einsum(
            "nkgd,nlkd->nkgl", query_head_count, key_head_count, preferred_element_type=jnp.float32
        )
        * score_scale
    )
    own_score = (
        jnp.einsum(
            "nkgd,nkd->nkg", query_head_count, incoming_key, preferred_element_type=jnp.float32
        )
        * score_scale
    )
    live_mask = jnp.arange(CACHE_SLOTS)[None, :] < cache_length[:, None]
    scores = jnp.where(live_mask[:, None, None, :], scores, -jnp.inf)
    row_max = jnp.maximum(jnp.max(scores, axis=-1), own_score)
    cache_terms = jnp.exp(scores - row_max[..., None])
    own_term = jnp.exp(own_score - row_max)
    row_total = jnp.sum(cache_terms, axis=-1) + own_term
    weights = (cache_terms / row_total[..., None]).astype(jnp.bfloat16)
    own_weight = (own_term / row_total).astype(jnp.bfloat16)
    mixed = jnp.einsum(
        "nkgl,nlkd->nkgd", weights, value_head_count, preferred_element_type=jnp.float32
    )
    mixed = (
        mixed
        + own_weight.astype(jnp.float32)[..., None]
        * incoming_value.astype(jnp.float32)[:, :, None, :]
    )
    return mixed.astype(jnp.bfloat16).reshape(count_of_rows, QUERY_HEADS * HEAD_SIZE)


MESH = pl.DeviceIdType.MESH


TILE = 256
WO_PIECES = 8
DOWN_LAG = 1


def layer_kernel(
    lengths,
    q_hbm,
    k_hbm,
    v_hbm,
    pair_hbm,
    hidden_hbm,
    gain_hbm,
    wo_hbm,
    wg_hbm,
    wd_hbm,
    out_ref,
    q_buf,
    k_buf,
    v_buf,
    pair_buf,
    hidden_buf,
    gain_buf,
    wo,
    wg,
    wd,
    q_rows,
    mixed,
    heads_all,
    heads_f32,
    proj_out,
    proj_in,
    residual,
    normed,
    squares,
    inverse,
    pre_part,
    pre_core,
    pre_sum,
    pre_send,
    pre_far,
    act,
    down_acc,
    down_out,
    down_in,
    load_sem,
    wo_sem,
    wg_sem,
    wd_sem,
    heads_send,
    heads_recv,
    proj_send,
    proj_recv,
    norm_send,
    norm_recv,
    square_send,
    square_recv,
    inverse_send,
    inverse_recv,
    core_send,
    core_recv,
    far_send,
    far_recv,
    act_send,
    act_recv,
    down_send,
    down_recv,
):
    n_blk, n_sum = lax.axis_size("blk"), lax.axis_size("sum")
    rows_here = q_buf.shape[0]
    units, columns = wd.shape
    tiles = units // TILE
    sizes = chunk_sizes(units)
    chunks = len(sizes)
    ends = [sum(sizes[: c + 1]) for c in range(chunks)]
    spans = [pl.ds(ends[c] - sizes[c], sizes[c]) for c in range(chunks)]
    b, s = lax.axis_index("blk"), lax.axis_index("sum")
    core = lax.rem(s, 2)
    core_peer = s + 1 - 2 * core
    far_peer = lax.rem(s + 2, n_sum)

    def blk_peer(k):
        return lax.rem(b + k, n_blk)

    def sum_peer(k):
        return lax.rem(s + k, n_sum)

    def send(src, dst, send_sem, recv_sem, where):
        return pltpu.make_async_remote_copy(
            src_ref=src,
            dst_ref=dst,
            send_sem=send_sem,
            recv_sem=recv_sem,
            device_id=where,
            device_id_type=MESH,
        )

    blk_order = [n_blk // 2] + [k for k in range(1, n_blk) if k != n_blk // 2]
    peers = [(i, j) for i in blk_order + [0] for j in (2, 3, 1, 0) if (i, j) != (0, 0)]

    barrier = pltpu.get_barrier_semaphore()
    first = [
        pltpu.make_async_copy(src, dst, load_sem.at[i])
        for i, (src, dst) in enumerate(
            [
                (q_hbm, q_buf),
                (k_hbm, k_buf),
                (pair_hbm, pair_buf),
                (v_hbm, v_buf),
                (hidden_hbm, hidden_buf),
                (gain_hbm, gain_buf),
            ]
        )
    ]

    def load_gate(t):
        span = pl.ds(pl.multiple_of(t * TILE, TILE), TILE)
        return pltpu.make_async_copy(wg_hbm.at[:, span, :], wg.at[:, span, :], wg_sem.at[t])

    def load_down(t):
        span = pl.ds(pl.multiple_of(t * TILE, TILE), TILE)
        return pltpu.make_async_copy(wd_hbm.at[span, :], wd.at[span, :], wd_sem.at[t])

    piece = wo.shape[0] // WO_PIECES
    load_out = [
        pltpu.make_async_copy(
            wo_hbm.at[pl.ds(i * piece, piece), :], wo.at[pl.ds(i * piece, piece), :], wo_sem.at[i]
        )
        for i in range(WO_PIECES)
    ]
    for copy in first[:4]:
        copy.start()
    for i, j in peers:
        pl.semaphore_signal(
            barrier,
            inc=1,
            device_id={"blk": blk_peer(i), "sum": sum_peer(j)},
            device_id_type=MESH,
        )
    first[0].wait()
    for copy in load_out + first[4:]:
        copy.start()
    for copy in first[1:4]:
        copy.wait()
    turns = turn_counts(tiles)

    def start_gate(t, carry):
        load_gate(t).start()
        return carry

    def start_down(t, carry):
        load_down(t).start()
        return carry

    lax.fori_loop(0, tiles, start_gate, 0)
    lax.fori_loop(0, tiles, start_down, 0)

    group = QUERY_HEADS // KEY_VALUE_HEADS
    queries = q_buf[...].astype(jnp.float32)
    for r in range(rows_here):
        for h in range(QUERY_HEADS):
            q_rows[r, h : h + 1, :] = queries[r : r + 1, h * HEAD_SIZE : (h + 1) * HEAD_SIZE]
    score_scale = HEAD_SIZE ** (-0.5)
    staged = []
    for r in range(rows_here):
        q32 = q_rows[r]
        q16 = q32.astype(jnp.bfloat16)
        new_key = pair_buf[r, 0:1, :].astype(jnp.float32)
        new_value = pair_buf[r, 1:2, :].astype(jnp.float32)
        scores, keys_new, values_new = [], [], []
        for j in range(KEY_VALUE_HEADS):
            cols = slice(j * HEAD_SIZE, (j + 1) * HEAD_SIZE)
            scores.append(
                lax.dot_general(
                    q16[j * group : (j + 1) * group],
                    k_buf[r, :, cols],
                    (((1,), (1,)), ((), ())),
                    preferred_element_type=jnp.float32,
                )
            )
            keys_new.append(jnp.broadcast_to(new_key[:, cols], (group, HEAD_SIZE)))
            values_new.append(jnp.broadcast_to(new_value[:, cols], (group, HEAD_SIZE)))
        scores = jnp.concatenate(scores, axis=0) * score_scale
        own = jnp.sum(q32 * jnp.concatenate(keys_new, axis=0), axis=1, keepdims=True) * score_scale
        staged.append((scores, own, jnp.concatenate(values_new, axis=0)))
    weighted = []
    for r in range(rows_here):
        scores, own, _ = staged[r]
        position = lax.broadcasted_iota(jnp.int32, scores.shape, 1)
        scores = jnp.where(position < lengths[r], scores, -jnp.inf)
        row_max = jnp.maximum(jnp.max(scores, axis=1, keepdims=True), own)
        terms = jnp.exp(scores - row_max)
        own_term = jnp.exp(own - row_max)
        total = jnp.sum(terms, axis=1, keepdims=True) + own_term
        weights = (terms / total).astype(jnp.bfloat16)
        weighted.append((weights, (own_term / total).astype(jnp.bfloat16).astype(jnp.float32)))
    for r in range(rows_here):
        weights, own_weight = weighted[r]
        outs = []
        for j in range(KEY_VALUE_HEADS):
            cols = slice(j * HEAD_SIZE, (j + 1) * HEAD_SIZE)
            outs.append(
                jnp.dot(
                    weights[j * group : (j + 1) * group],
                    v_buf[r, :, cols],
                    preferred_element_type=jnp.float32,
                )
            )
        result = jnp.concatenate(outs, axis=0) + own_weight * staged[r][2]
        mixed[r] = result.astype(jnp.bfloat16).reshape(mixed.shape[1:])

    pl.semaphore_wait(barrier, len(peers))
    moves = []
    for n, (i, j) in enumerate(peers):
        moves.append(
            send(
                mixed.at[:, blk_peer(i)],
                heads_all.at[b, s],
                heads_send.at[n],
                heads_recv.at[n],
                {"blk": blk_peer(i), "sum": sum_peer(j)},
            )
        )
    for copy in moves:
        copy.start()
    heads_all[b, s] = mixed[:, b]

    def turn(t, carry):
        load_gate(t).wait()
        span = pl.ds(pl.multiple_of(t * TILE, TILE), TILE)
        for g in range(2):
            for f in range(columns // TILE):
                cols = slice(f * TILE, (f + 1) * TILE)
                wg[g, span, cols] = wg[g, span, cols].T
        return carry

    lax.fori_loop(0, turns[0], turn, 0)
    for n, (i, j) in enumerate(peers):
        moves[n].wait_send()
        other_b, other_s = lax.rem(b + n_blk - i, n_blk), lax.rem(s + n_sum - j, n_sum)
        send(
            mixed.at[:, blk_peer(i)],
            heads_all.at[other_b, other_s],
            heads_send.at[n],
            heads_recv.at[n],
            {"blk": blk_peer(i), "sum": sum_peer(j)},
        ).wait_recv()
    heads_f32[...] = heads_all[...].astype(jnp.float32).reshape(heads_f32.shape)
    per_block = wo.shape[0] // HEAD_SIZE
    rows_all = n_blk * n_sum * rows_here
    picked = jnp.concatenate(
        [
            heads_f32[pl.ds(h, rows_all, stride=per_block), :].astype(jnp.bfloat16)
            for h in range(per_block)
        ],
        axis=1,
    )
    for copy in load_out:
        copy.wait()
    parts = column_parts(columns)
    moves = []
    for p, (first_col, width) in enumerate(parts):
        cols = pl.ds(first_col, width)
        projected = jnp.dot(picked, wo[:, cols], preferred_element_type=jnp.float32)
        proj_out[:, :, cols] = projected.reshape(n_blk, -1, width).astype(jnp.bfloat16)
        moves.append(
            [
                send(
                    proj_out.at[blk_peer(k), :, cols],
                    proj_in.at[k - 1, :, cols],
                    proj_send.at[p * (n_blk - 1) + k - 1],
                    proj_recv.at[p * (n_blk - 1) + k - 1],
                    {"blk": blk_peer(k)},
                )
                for k in range(1, n_blk)
            ]
        )
        for k in blk_order:
            moves[p][k - 1].start()
    lax.fori_loop(turns[0], turns[1], turn, 0)
    first[4].wait()
    first[5].wait()
    norm_moves = []
    square_sum = 0.0
    for p, (first_col, width) in enumerate(parts):
        cols = pl.ds(first_col, width)
        total = hidden_buf[:, cols] + proj_out[b, :, cols].astype(jnp.float32)
        for k in range(1, n_blk):
            moves[p][k - 1].wait()
            total = total + proj_in[k - 1, :, cols].astype(jnp.float32)
        residual[:, cols] = total
        scaled = [
            total[:, n : n + 128] * gain_buf[(first_col + n) // 128 : (first_col + n) // 128 + 1, :]
            for n in range(0, width, 128)
        ]
        normed[b, :, cols] = jnp.concatenate(scaled, axis=1).astype(jnp.bfloat16)
        norm_moves.append(
            [
                send(
                    normed.at[b, :, cols],
                    normed.at[b, :, cols],
                    norm_send.at[p * (n_blk - 1) + k - 1],
                    norm_recv.at[p * (n_blk - 1) + k - 1],
                    {"blk": blk_peer(k)},
                )
                for k in range(1, n_blk)
            ]
        )
        for k in blk_order:
            norm_moves[p][k - 1].start()
        square_sum = square_sum + jnp.sum(total * total, axis=1, keepdims=True)
    squares[s] = jnp.broadcast_to(square_sum, squares.shape[1:])
    square_moves = [
        send(
            squares.at[s],
            squares.at[s],
            square_send.at[k - 1],
            square_recv.at[k - 1],
            {"sum": sum_peer(k)},
        )
        for k in range(1, n_sum)
    ]
    for copy in square_moves:
        copy.start()

    def settle(copies, buffer, send_sems, recv_sems):
        for k in range(1, n_blk):
            copies[k - 1].wait_send()
            other = lax.rem(b + n_blk - k, n_blk)
            send(
                buffer.at[other],
                buffer.at[other],
                send_sems.at[k - 1],
                recv_sems.at[k - 1],
                {"blk": blk_peer(k)},
            ).wait_recv()

    lax.fori_loop(turns[1], tiles, turn, 0)
    for k in range(1, n_sum):
        square_moves[k - 1].wait_send()
        other = lax.rem(s + n_sum - k, n_sum)
        send(
            squares.at[other],
            squares.at[other],
            square_send.at[k - 1],
            square_recv.at[k - 1],
            {"sum": sum_peer(k)},
        ).wait_recv()
    inverse[b] = lax.rsqrt(jnp.sum(squares[...], axis=0) / D + 1e-06)
    inverse_moves = [
        send(
            inverse.at[b],
            inverse.at[b],
            inverse_send.at[k - 1],
            inverse_recv.at[k - 1],
            {"blk": blk_peer(k)},
        )
        for k in range(1, n_blk)
    ]
    for copy in inverse_moves:
        copy.start()
    for p, (first_col, width) in enumerate(parts):
        for k in range(1, n_blk):
            norm_moves[p][k - 1].wait_send()
            there = normed.at[lax.rem(b + n_blk - k, n_blk), :, pl.ds(first_col, width)]
            n = p * (n_blk - 1) + k - 1
            send(there, there, norm_send.at[n], norm_recv.at[n], {"blk": blk_peer(k)}).wait_recv()
    features = normed[...].astype(jnp.float32).reshape(rows_all, columns).astype(jnp.bfloat16)
    half = rows_all // 2
    to_core = [
        send(
            pre_part.at[1 - core, spans[c]],
            pre_core.at[spans[c]],
            core_send.at[c],
            core_recv.at[c],
            {"sum": core_peer},
        )
        for c in range(chunks)
    ]
    to_far = [
        send(
            pre_send.at[spans[c]],
            pre_far.at[spans[c]],
            far_send.at[c],
            far_recv.at[c],
            {"sum": far_peer},
        )
        for c in range(chunks)
    ]
    spread = [
        send(
            act.at[core, spans[c]],
            act.at[core, spans[c]],
            act_send.at[c],
            act_recv.at[c],
            {"sum": core_peer},
        )
        for c in range(chunks)
    ]

    def gate_tile(t):
        u = t * TILE
        for g in range(2):
            turned = jnp.concatenate(
                [wg[g, u : u + TILE, f : f + TILE] for f in range(0, columns, TILE)], axis=0
            )
            value = jnp.dot(features, turned, preferred_element_type=jnp.float32)
            value = value.astype(jnp.bfloat16)
            pre_part[0, t, g] = value[:half]
            pre_part[1, t, g] = value[half:]

    def core_part(c):
        to_core[c].wait()
        added = pre_part[core, spans[c]].astype(jnp.float32) + pre_core[spans[c]].astype(
            jnp.float32
        )
        pre_sum[spans[c]] = added
        pre_send[spans[c]] = added.astype(jnp.bfloat16)
        to_far[c].start()

    def act_part(c):
        to_far[c].wait()
        total = pre_sum[spans[c]] + pre_far[spans[c]].astype(jnp.float32)
        gate = total[:, 0] * factor
        up = total[:, 1] * factor
        act[core, spans[c]] = (gate / (1.0 + jnp.exp(-gate)) * up).astype(jnp.bfloat16)
        spread[c].start()

    def down_part(c):
        spread[c].wait_send()
        send(
            act.at[1 - core, spans[c]],
            act.at[1 - core, spans[c]],
            act_send.at[c],
            act_recv.at[c],
            {"sum": core_peer},
        ).wait_recv()
        span = range(ends[c] - sizes[c], ends[c])
        for t in span:
            load_down(t).wait()
        value = jnp.dot(
            jnp.concatenate([act[:, t].reshape(rows_all, TILE) for t in span], axis=1),
            wd[pl.ds(span[0] * TILE, sizes[c] * TILE), :],
            preferred_element_type=jnp.float32,
        )
        if c > 0:
            value = value + down_acc[...]
        down_acc[...] = value

    ready = 0
    for t in range(tiles):
        gate_tile(t)
        if t + 1 in ends:
            done = ends.index(t + 1)
            to_core[done].start()
            if done >= 1:
                core_part(done - 1)
                ready = done
    for c in range(ready, chunks):
        core_part(c)
    settle(inverse_moves, inverse, inverse_send, inverse_recv)
    factor = inverse[pl.ds((n_blk // 2) * core, n_blk // 2)].reshape(half, 128)[:, :1]
    for step in range(chunks + DOWN_LAG):
        if step < chunks:
            act_part(step)
        if step >= DOWN_LAG:
            down_part(step - DOWN_LAG)
    down_out[...] = down_acc[...].reshape(down_out.shape).astype(jnp.bfloat16)
    moves = [
        send(
            down_out.at[blk_peer(k)],
            down_in.at[k - 1],
            down_send.at[k - 1],
            down_recv.at[k - 1],
            {"blk": blk_peer(k)},
        )
        for k in range(1, n_blk)
    ]
    for k in blk_order:
        moves[k - 1].start()
    total = residual[...] + down_out[b].astype(jnp.float32)
    for k in range(1, n_blk):
        moves[k - 1].wait()
        total = total + down_in[k - 1].astype(jnp.float32)
    out_ref[...] = total


def column_parts(columns):
    first = TILE * -(-columns // (2 * TILE))
    return [(0, first), (first, columns - first)]


def turn_counts(tiles):
    return [2 * tiles // 5, 16 * tiles // 25]


def chunk_sizes(units):
    tiles = units // TILE
    first, last = [3], [3]
    middle = tiles - sum(first + last)
    parts = -(-middle // 5)
    sizes = [middle // parts + (i < middle % parts) for i in range(parts)]
    return first + sizes + last


def kernel_fits(queries, hidden, out_weight, gate_up_weight):
    n_blk, n_sum = lax.axis_size("blk"), lax.axis_size("sum")
    units, columns = gate_up_weight.shape[1:]
    weights = 2 * (out_weight.size + gate_up_weight.size + units * columns)
    return (
        n_sum == 4
        and n_blk % 2 == 0
        and queries.shape[0] == 2
        and hidden.shape[0] == 8
        and out_weight.shape[0] % (16 * HEAD_SIZE) == 0
        and units % 256 == 0
        and units >= 13 * 256
        and columns % 256 == 0
        and columns >= 512
        and weights <= 53 * 2**20
    )


def layer_in_kernel(
    queries,
    cached_key_rows,
    cached_value_rows,
    incoming_pairs,
    cache_length,
    hidden,
    norm_gain,
    out_weight,
    gate_up_weight,
    down_weight,
):
    n_blk, n_sum = lax.axis_size("blk"), lax.axis_size("sum")
    rows = queries.shape[0]
    own_rows, columns = hidden.shape
    rows_all = n_blk * own_rows
    units = down_weight.shape[0]
    chunks = len(chunk_sizes(units))
    per_block = out_weight.shape[0] // HEAD_SIZE
    bf16, f32 = jnp.bfloat16, jnp.float32
    anywhere = pl.BlockSpec(memory_space=pl.ANY)
    tiles = units // TILE
    sems = [6, WO_PIECES, tiles, tiles]
    sems += [n_blk * n_sum - 1] * 2 + [2 * (n_blk - 1)] * 4 + [n_sum - 1] * 2
    sems += [n_blk - 1] * 2 + [chunks] * 6 + [n_blk - 1] * 2
    gain = norm_gain.reshape(columns // 128, 128)
    like = lambda x: pltpu.VMEM(x.shape, x.dtype)
    half = rows_all // 2
    return pl.pallas_call(
        layer_kernel,
        out_shape=pltpu.VMEM(hidden.shape, f32),
        in_specs=[pl.BlockSpec(memory_space=pltpu.SMEM)] + [anywhere] * 9,
        out_specs=pl.BlockSpec(memory_space=pltpu.VMEM),
        scratch_shapes=[
            like(queries),
            like(cached_key_rows),
            like(cached_value_rows),
            like(incoming_pairs),
            like(hidden),
            like(gain),
            like(out_weight),
            like(gate_up_weight),
            like(down_weight),
            pltpu.VMEM((rows, QUERY_HEADS, HEAD_SIZE), f32),
            pltpu.VMEM((rows, n_blk, per_block, HEAD_SIZE), bf16),
            pltpu.VMEM((n_blk, n_sum, rows, per_block, HEAD_SIZE), bf16),
            pltpu.VMEM((rows_all * per_block, HEAD_SIZE), f32),
            pltpu.VMEM((n_blk, own_rows, columns), bf16),
            pltpu.VMEM((n_blk - 1, own_rows, columns), bf16),
            pltpu.VMEM(hidden.shape, f32),
            pltpu.VMEM((n_blk, own_rows, columns), bf16),
            pltpu.VMEM((n_sum, own_rows, 128), f32),
            pltpu.VMEM((n_blk, own_rows, 128), f32),
            pltpu.VMEM((2, tiles, 2, half, TILE), bf16),
            pltpu.VMEM((tiles, 2, half, TILE), bf16),
            pltpu.VMEM((tiles, 2, half, TILE), f32),
            pltpu.VMEM((tiles, 2, half, TILE), bf16),
            pltpu.VMEM((tiles, 2, half, TILE), bf16),
            pltpu.VMEM((2, tiles, half, TILE), bf16),
            pltpu.VMEM((rows_all, columns), f32),
            pltpu.VMEM((n_blk, own_rows, columns), bf16),
            pltpu.VMEM((n_blk - 1, own_rows, columns), bf16),
        ]
        + [pltpu.SemaphoreType.DMA((n,)) for n in sems],
        compiler_params=pltpu.CompilerParams(
            collective_id=0, has_side_effects=True, vmem_limit_bytes=60 * 2**20
        ),
    )(
        cache_length,
        queries,
        cached_key_rows,
        cached_value_rows,
        incoming_pairs,
        hidden,
        gain,
        out_weight,
        gate_up_weight,
        down_weight,
    )


def on_device(
    queries,
    cached_key_rows,
    cached_value_rows,
    incoming_pairs,
    cache_length,
    hidden,
    norm_gain,
    out_weight,
    gate_up_weight,
    down_weight,
):
    if kernel_fits(queries, hidden, out_weight, gate_up_weight):
        return layer_in_kernel(
            queries,
            cached_key_rows,
            cached_value_rows,
            incoming_pairs,
            cache_length,
            hidden,
            norm_gain,
            out_weight,
            gate_up_weight,
            down_weight,
        )
    attended = attend_padded(
        queries, cached_key_rows, cached_value_rows, incoming_pairs, cache_length
    )
    spread = lax.all_to_all(attended, "blk", split_axis=1, concat_axis=0, tiled=True)
    spread = spread.reshape(lax.axis_size("blk"), attended.shape[0], spread.shape[1])
    heads_rows = lax.all_gather(spread, "sum", axis=1, tiled=True).reshape(-1, spread.shape[2])
    picked = heads_rows
    projected = lax.psum_scatter(
        jnp.dot(picked, out_weight, preferred_element_type=jnp.float32).astype(jnp.bfloat16),
        "blk",
        scatter_dimension=0,
        tiled=True,
    ).astype(jnp.float32)
    residual = hidden + projected
    square_sum = lax.psum(jnp.sum(residual * residual, axis=1), "sum")
    inverse = lax.rsqrt(square_sum / D + 1e-06)
    normed = (residual * inverse[:, None] * norm_gain[None, :]).astype(jnp.bfloat16)
    pre_terms = jnp.einsum(
        "nd,gfd->ngf",
        lax.all_gather(normed, "blk", axis=0, tiled=True),
        gate_up_weight,
        preferred_element_type=jnp.float32,
    )
    summed = lax.psum(pre_terms.astype(jnp.bfloat16), "sum").astype(jnp.float32)
    activated = (jax.nn.silu(summed[:, 0]) * summed[:, 1]).astype(jnp.bfloat16)
    picked = activated
    feed_sum = lax.psum_scatter(
        jnp.dot(picked, down_weight, preferred_element_type=jnp.float32).astype(jnp.bfloat16),
        "blk",
        scatter_dimension=0,
        tiled=True,
    ).astype(jnp.float32)
    return residual + feed_sum


def solution(mesh):
    placed = (
        P(("groups", "blk", "sum"), None),
        P(("groups", "blk", "sum"), None, None),
        P(("groups", "blk", "sum"), None, None),
        P(("groups", "blk", "sum"), None, None),
        P(("groups", "blk", "sum")),
        P(("groups", "blk"), "sum"),
        P("sum"),
        P("blk", "sum"),
        P(None, "blk", "sum"),
        P("blk", "sum"),
    )
    return jax.shard_map(
        on_device,
        mesh=mesh,
        in_specs=placed,
        out_specs=P(("groups", "blk"), "sum"),
        check_vma=False,
    )
```
